32 devices in a mesh: gx: 16 (over z, y, core), ga: 2 (over x).
Axes of the slice: x: 2, y: 2, z: 4, core: 2. Of those that a mesh axis runs over, the one named last changes fastest.
Arguments:
- velocity: float32 [6144, 4096], P('gx', 'ga'), may hold values from -12 to 12, as said below
- left_gram: float32 [25, 5], replicated, may hold values from -2.5 to 2.5
- right_gram: float32 [25, 5], replicated, may hold values from -2.5 to 2.5
Outputs:
- x_slope: float32 [6144, 4096], P('gx', 'ga')
- section_field: float32 [6144, 4096], P('gx', 'ga')
The draws below stay inside these ranges and needn't reach their ends.
Inputs may be any that keep to these rules, and one draw needn't show every extreme that they name: velocity at the grid points.
All inputs are finite; a program needn't handle non-finite values.
Results may differ from the reference program's by a relative error of at most 0.000071.
Values sent between devices are 32-bit elements; how exact they have to be, the bound alone decides.
No kernel may reach another device: no remote copies, remote signals or barrier semaphores. Data moves between devices by JAX's collectives and lax.ppermute only.
A program may use at most 64 MiB of HBM per device.

```python
import math
import jax
import jax.numpy as jnp
from jax import lax

CONT = 25
DG = 5
NX = 6144
LINES = 4096


def draw_velocity(key, part):
    position = jnp.arange(NX, dtype=jnp.float32)[:, None] / NX
    line_pos = jnp.arange(LINES, dtype=jnp.float32)[None, :] / LINES
    noise = jnp.clip(jax.random.normal(key, (NX, LINES), jnp.float32), -5.0, 5.0)
    amplitude = 0.6 * (1.0 + position) * (1.0 + line_pos)
    return amplitude * noise


def normal_values(stream_key, extent, scale, most, kind=jnp.bfloat16):
    entries = scale * jax.random.normal(stream_key, extent, jnp.float32)
    return jnp.clip(entries, min=-most, max=most).astype(kind)


def setup_inputs(seed: int = 0) -> dict:
    key_list = jax.random.split(jax.random.key(seed), 4)
    return {
        "velocity": draw_velocity(jax.random.fold_in(key_list[3], 71), 0),
        "left_gram": normal_values(key_list[1], (CONT, DG), DG ** -0.5, 2.5, jnp.float32),
        "right_gram": normal_values(key_list[2], (CONT, DG), DG ** -0.5, 2.5, jnp.float32),
    }


courant = 0.5
epsilon = 1e-06

def line_slope(extended):
    period = extended.shape[0]
    spectrum = jnp.fft.rfft(extended, axis=0)
    wavenumber = jnp.arange(spectrum.shape[0], dtype=jnp.float32) * (2.0 * jnp.pi / period)
    slope_all = jnp.fft.irfft(spectrum * (1j * wavenumber)[:, None], n=period, axis=0)
    return slope_all[:NX]

def reference(velocity, left_gram, right_gram):
    line_total = velocity.shape[1]
    block_size = math.gcd(line_total, 512)
    num_blocks = line_total // block_size
    hp = lax.Precision.HIGHEST

    def one_block(which):
        window = lax.dynamic_slice_in_dim(velocity, which * block_size, block_size, 1)
        extension = jnp.dot(left_gram, window[:DG], precision=hp, preferred_element_type=jnp.float32)
        extension = extension + jnp.dot(right_gram, window[NX - DG:], precision=hp, preferred_element_type=jnp.float32)
        extended = jnp.concatenate([window, extension], axis=0)
        return line_slope(extended)
    pieces = lax.map(one_block, jnp.arange(num_blocks, dtype=jnp.int32))
    x_slope = jnp.transpose(pieces, (1, 0, 2)).reshape(NX, line_total)
    mean_square = jnp.mean(velocity * velocity)
    advect_rate = courant / jnp.sqrt(mean_square + epsilon)
    section_field = velocity - advect_rate * velocity * x_slope
    return (x_slope, section_field)
```

```python
import math

import jax
import jax.numpy as jnp
import numpy as np
from jax import lax
from jax.experimental import pallas as pl
from jax.experimental.pallas import tpu as pltpu
from jax.sharding import PartitionSpec as P

courant = 0.5
epsilon = 1e-06
BLOCK = 128
LANE = 128
BF = jnp.bfloat16
F32 = jnp.float32


def round_up(value, step):
    return -(-value // step) * step


def kernel_values(period, row_total, depth):
    offset = row_total - np.arange(row_total + depth, dtype=np.int64)
    wrapped = (offset + period // 2) % period - period // 2
    safe = np.where(wrapped == 0, 1, wrapped)
    sign = np.where(safe % 2 == 0, 1.0, -1.0)
    values = sign * (math.pi / period) / np.sin(math.pi * safe / period)
    return np.where(wrapped == 0, 0.0, values).astype(np.float32)


def toeplitz_tables(values, width):
    step = 512
    near_at = width - values.shape[1] + BLOCK

    def body(w_ref, high_ref, mid_ref):
        def fill(j, _):
            at = pl.multiple_of(j * step, step)
            lane = w_ref[:, pl.ds(at, step + BLOCK)]
            rows = jnp.broadcast_to(lane, (BLOCK, step + BLOCK))
            rows = pltpu.roll(rows, 0, 1, stride=1, stride_axis=0)[:, BLOCK:]
            high = rows.astype(BF)
            high_ref[:, pl.ds(at, step)] = high
            mid_ref[:, pl.ds(at, step)] = (rows - high.astype(F32)).astype(BF)
            return 0

        lax.fori_loop(0, width // step, fill, 0)

    return pl.pallas_call(
        body,
        name="toeplitz_tables",
        out_shape=[jax.ShapeDtypeStruct((BLOCK, width), BF)] * 2,
        cost_estimate=pl.CostEstimate(
            flops=BLOCK * width * 8, bytes_accessed=BLOCK * width * 4, transcendentals=0
        ),
    )(values)


def split_blocks(velocity, count):
    rows, lines = velocity.shape
    width = lines // count

    def body(v_ref, b_ref, s_ref):
        @pl.when(pl.program_id(0) == 0)
        def _():
            s_ref[...] = jnp.zeros_like(s_ref)

        part = v_ref[...]
        b_ref[0] = part
        s_ref[...] += jnp.sum((part * part).reshape(rows // 8, 8, width), axis=0)

    return pl.pallas_call(
        body,
        name="split_blocks",
        grid=(count,),
        in_specs=[pl.BlockSpec((rows, width), lambda i: (0, i))],
        out_specs=[
            pl.BlockSpec((1, rows, width), lambda i: (i, 0, 0)),
            pl.BlockSpec((8, width), lambda i: (0, 0)),
        ],
        out_shape=[
            jax.ShapeDtypeStruct((count, rows, width), F32),
            jax.ShapeDtypeStruct((8, width), F32),
        ],
        cost_estimate=pl.CostEstimate(
            flops=rows * lines * 2, bytes_accessed=rows * lines * 8, transcendentals=0
        ),
    )(velocity)


def line_slopes(lines_in, gram, high, mid, cont, match):
    total, width = lines_in.shape
    depth = round_up(total + cont, LANE)
    ext_rows = depth - total
    block_count = total // BLOCK

    def body(x_ref, g_ref, high_ref, mid_ref, o_ref, both):
        @pl.when(pl.program_id(0) == 0)
        def _():
            def put(at, size, part):
                top = part.astype(BF)
                both[pl.ds(at, size), :width] = top
                both[pl.ds(at, size), width:] = (part - top.astype(F32)).astype(BF)

            def fill(j, _):
                at = pl.multiple_of(j * BLOCK, BLOCK)
                put(at, BLOCK, x_ref[pl.ds(at, BLOCK), :])
                return 0

            lax.fori_loop(0, block_count, fill, 0)
            ext = jnp.zeros((ext_rows, width), F32)
            for j in range(match):
                ext += g_ref[:, j : j + 1] * x_ref[j : j + 1, :]
            for j in range(match):
                row = total - match + j
                ext += g_ref[:, match + j : match + j + 1] * x_ref[row : row + 1, :]
            put(total, ext_rows, ext)

        block = pl.program_id(0)
        at = pl.multiple_of((block_count - 1 - block) * BLOCK, BLOCK)
        first = jnp.dot(high_ref[:, pl.ds(at, depth)], both[...], preferred_element_type=F32)
        second = jnp.dot(mid_ref[:, pl.ds(at, depth)], both[...], preferred_element_type=F32)
        o_ref[...] = (first[:, :width] + (first[:, width:] + second[:, :width])) + second[:, width:]

    return pl.pallas_call(
        body,
        name="line_slopes",
        grid=(block_count,),
        in_specs=[pl.BlockSpec(memory_space=pltpu.VMEM)] * 4,
        out_specs=pl.BlockSpec((BLOCK, width), lambda i: (i, 0)),
        out_shape=jax.ShapeDtypeStruct((total, width), F32),
        scratch_shapes=[pltpu.VMEM((depth, 2 * width), BF)],
        cost_estimate=pl.CostEstimate(
            flops=8 * total * depth * width, bytes_accessed=8 * total * width, transcendentals=0
        ),
    )(lines_in, gram, high, mid)


def advect(velocity, returned, rate):
    rows, lines = velocity.shape
    count, _, width = returned.shape

    def body(rate_ref, v_ref, r_ref, s_ref, f_ref):
        slope = r_ref[0]
        field = v_ref[...]
        s_ref[...] = slope
        f_ref[...] = field - rate_ref[0, 0] * field * slope

    tile = pl.BlockSpec((rows, width), lambda i: (0, i))
    return pl.pallas_call(
        body,
        name="advect",
        grid=(count,),
        in_specs=[
            pl.BlockSpec(memory_space=pltpu.SMEM),
            tile,
            pl.BlockSpec((1, rows, width), lambda i: (i, 0, 0)),
        ],
        out_specs=[tile, tile],
        out_shape=[jax.ShapeDtypeStruct((rows, lines), F32)] * 2,
        cost_estimate=pl.CostEstimate(
            flops=rows * lines * 3, bytes_accessed=rows * lines * 16, transcendentals=0
        ),
    )(rate, velocity, returned)


def total_over(part, axis):
    size = lax.axis_size(axis)
    if size & (size - 1):
        moving = part
        for _ in range(size - 1):
            moving = lax.ppermute(moving, axis, [(i, (i + 1) % size) for i in range(size)])
            part = part + moving
        return part
    step = 1
    while step < size:
        part = part + lax.ppermute(part, axis, [(i, i ^ step) for i in range(size)])
        step *= 2
    return part


def per_device(velocity, left_gram, right_gram):
    row_count, line_total = velocity.shape
    cont, match = left_gram.shape
    gx_count = lax.axis_size("gx")
    ga_count = lax.axis_size("ga")
    total = row_count * gx_count
    width = line_total // gx_count
    depth = round_up(total + cont, LANE)
    table_width = total - BLOCK + depth

    blocks, sums = split_blocks(velocity, gx_count)
    owned = lax.all_to_all(blocks, "gx", split_axis=0, concat_axis=0, tiled=True)
    values = jnp.asarray(kernel_values(total + cont, total, depth))[None, :]
    high, mid = toeplitz_tables(values, table_width)
    energy = total_over(total_over(sums, "ga"), "gx")
    mean_square = jnp.sum(energy) / (row_count * line_total * gx_count * ga_count)
    advect_rate = (courant / jnp.sqrt(mean_square + epsilon)).reshape(1, 1)

    gram = jnp.concatenate([left_gram, right_gram], axis=1)
    gram = jnp.pad(gram, ((0, depth - total - cont), (0, 0)))
    slopes = line_slopes(owned.reshape(total, width), gram, high, mid, cont, match)
    returned = lax.all_to_all(
        slopes.reshape(gx_count, row_count, width), "gx", split_axis=0, concat_axis=0, tiled=True
    )
    return tuple(advect(velocity, returned, advect_rate))


def solution(mesh):
    return jax.shard_map(
        per_device,
        mesh=mesh,
        in_specs=(P("gx", "ga"), P(), P()),
        out_specs=(P("gx", "ga"), P("gx", "ga")),
        check_vma=False,
    )
```

```python
import math

import jax
import jax.numpy as jnp
import numpy as np
from jax import lax
from jax.experimental import pallas as pl
from jax.experimental.pallas import tpu as pltpu
from jax.sharding import PartitionSpec as P

courant = 0.5
epsilon = 1e-06
BLOCK = 128
LANE = 128
GROUP = 8
PARTS = 3
BF = jnp.bfloat16
F32 = jnp.float32


def add(a, b):
    return b if a is None else a if b is None else a + b


def sub(a, b):
    return a if b is None else -b if a is None else a - b


def scale(a, c):
    return None if a is None else a * np.float32(c)


def turn(value, angle):
    c, s = math.cos(angle), math.sin(angle)
    re, im = value
    return (sub(scale(re, c), scale(im, s)), add(scale(im, c), scale(re, s)))


def real_transform(seq):
    size = len(seq)
    if size == 1:
        return [(seq[0], None)]
    if size == 3:
        far = add(seq[1], seq[2])
        gap = sub(seq[1], seq[2])
        return [
            (add(seq[0], far), None),
            (sub(seq[0], scale(far, 0.5)), scale(gap, -math.sqrt(0.75))),
        ]
    even = real_transform(seq[0::2])
    odd = real_transform(seq[1::2])
    out = [None] * (size // 2 + 1)
    for f in range((size + 3) // 4):
        e = even[f]
        o = odd[f] if f == 0 else turn(odd[f], -2.0 * math.pi * f / size)
        out[f] = (add(e[0], o[0]), add(e[1], o[1]))
        out[size // 2 - f] = (sub(e[0], o[0]), sub(o[1], e[1]))
    if size % 4 == 0:
        f = size // 4
        out[f] = (even[f][0], scale(odd[f][0], -1.0))
    return out


def real_inverse(spec, size, count):
    if count <= 0:
        return []
    if size == 1:
        return [spec[0][0]]
    if size == 3:
        out = [add(spec[0][0], spec[1][0])]
        if count > 1:
            base = sub(spec[0][0], scale(spec[1][0], 0.5))
            side = scale(spec[1][1], math.sqrt(0.75))
            out.append(sub(base, side))
            out.append(add(base, side))
        return out[:count]
    half = size // 2
    even = [None] * (half // 2 + 1)
    odd = [None] * (half // 2 + 1)
    for f in range((size + 3) // 4):
        a, b = spec[f], spec[half - f]
        even[f] = (add(a[0], b[0]), sub(a[1], b[1]))
        diff = (sub(a[0], b[0]), add(a[1], b[1]))
        odd[f] = diff if f == 0 else turn(diff, 2.0 * math.pi * f / size)
    if size % 4 == 0:
        f = size // 4
        even[f] = (spec[f][0], None)
        odd[f] = (scale(spec[f][1], -1.0), None)
    first = real_inverse(even, half, (count + 1) // 2)
    second = real_inverse(odd, half, count // 2)
    out = [None] * count
    out[0::2] = first
    out[1::2] = second
    return out


def transform_size(least):
    size = 1
    while True:
        if size >= least:
            return size
        if size % 2 == 0 and size // 2 * 3 >= least:
            return size // 2 * 3
        size *= 2


def slope_spectrum(period, out_blocks, in_blocks, size):
    offsets = np.arange(size)
    offsets = np.where(offsets < out_blocks, offsets, offsets - size)
    step = np.arange(2 * BLOCK)
    index = BLOCK * offsets[:, None] + BLOCK - step[None, :]
    wrapped = (index + period // 2) % period - period // 2
    safe = np.where(wrapped == 0, 1, wrapped)
    sign = np.where(safe % 2 == 0, 1.0, -1.0)
    values = sign * (math.pi / period) / np.sin(math.pi * safe / period)
    values = np.where(wrapped == 0, 0.0, values)
    spectrum = np.fft.fft(values, axis=0)[: size // 2 + 1] / size
    table = np.empty((size, 2 * BLOCK))
    table[0] = spectrum[0].real
    table[1] = spectrum[size // 2].real
    table[2::2] = 2.0 * spectrum[1 : size // 2].real
    table[3::2] = 2.0 * spectrum[1 : size // 2].imag
    return table.astype(np.float32)


def split_parts(value, parts):
    out = []
    for _ in range(parts - 1):
        top = value.astype(BF)
        out.append(top)
        value = value - top.astype(F32)
    out.append(value.astype(BF))
    return out


def toeplitz_tables(spectrum):
    slots = spectrum.shape[0] // 2

    def body(w_ref, o_ref):
        def fill(f, _):
            for side in range(2):
                lane = w_ref[pl.ds(2 * f + side, 1), :]
                rows = jnp.broadcast_to(lane, (BLOCK, 2 * BLOCK))
                rows = pltpu.roll(rows, 0, 1, stride=1, stride_axis=0)[:, BLOCK:]
                for p, part in enumerate(split_parts(rows, PARTS)):
                    o_ref[f, p * BLOCK : (p + 1) * BLOCK, side * BLOCK : (side + 1) * BLOCK] = part
            return 0

        lax.fori_loop(0, slots, fill, 0)

    return pl.pallas_call(
        body,
        name="toeplitz_tables",
        out_shape=jax.ShapeDtypeStruct((slots, PARTS * BLOCK, 2 * BLOCK), BF),
        cost_estimate=pl.CostEstimate(
            flops=slots * BLOCK * BLOCK * 32,
            bytes_accessed=slots * PARTS * BLOCK * BLOCK * 4,
            transcendentals=0,
        ),
    )(spectrum)


def pack(velocity, place, count):
    rows, lines = velocity.shape
    width = lines // count
    steps = 8
    chunk = rows // steps

    def body(place_ref, v_ref, *refs):
        outs, sums = refs[:-1], refs[-1]
        step = pl.program_id(0)
        at = pl.multiple_of(step * chunk, 8)

        @pl.when(step == 0)
        def _():
            sums[...] = jnp.zeros_like(sums)

        total = sums[...]
        for k in range(count):
            lane = pl.multiple_of(lax.rem(place_ref[0] + k, count) * width, LANE)
            part = v_ref[:, pl.ds(lane, width)]
            outs[k][pl.ds(at, chunk), :] = part
            total += jnp.sum((part * part).reshape(chunk // 8, 8, width), axis=0)
        sums[...] = total

        @pl.when(step == steps - 1)
        def _():
            for k in range(count):
                outs[k][rows:, :] = total

    return pl.pallas_call(
        body,
        name="pack",
        grid=(steps,),
        in_specs=[
            pl.BlockSpec(memory_space=pltpu.SMEM),
            pl.BlockSpec((chunk, lines), lambda i: (i, 0)),
        ],
        out_specs=[pl.BlockSpec((rows + 8, width), lambda i: (0, 0))] * count,
        out_shape=[jax.ShapeDtypeStruct((rows + 8, width), F32)] * count,
        scratch_shapes=[pltpu.VMEM((8, width), F32)],
        cost_estimate=pl.CostEstimate(
            flops=rows * lines * 2, bytes_accessed=rows * lines * 8, transcendentals=0
        ),
    )(place, velocity)


def line_slopes(pieces, place, gram, tables, cont, match):
    count = len(pieces)
    rows = pieces[0].shape[0] - 8
    width = pieces[0].shape[1]
    total = rows * count
    out_blocks = total // BLOCK
    in_blocks = -(-(total + cont) // BLOCK)
    size = 2 * tables.shape[0]
    ext_rows = in_blocks * BLOCK - total

    def body(place_ref, g_ref, t_ref, *refs):
        ins, outs = refs[:count], refs[count : 2 * count]
        energy_ref, lines, spec, tiles, in_sem, sum_sem, out_sem = refs[2 * count :]

        def arrive(k):
            at = pl.multiple_of(lax.rem(place_ref[0] + count - k, count) * rows, 8)
            return pltpu.make_async_copy(
                ins[k].at[pl.ds(0, rows)], lines.at[pl.ds(at, rows)], in_sem.at[k]
            )

        def arrive_sum(k):
            return pltpu.make_async_copy(ins[k].at[pl.ds(rows, 8)], tiles.at[k], sum_sem.at[k])

        def leave(k):
            at = pl.multiple_of(lax.rem(place_ref[0] + k, count) * rows, 8)
            return pltpu.make_async_copy(lines.at[pl.ds(at, rows)], outs[k], out_sem.at[k])

        for k in range(count):
            arrive(k).start()
            arrive_sum(k).start()
        for k in range(count):
            arrive(k).wait()
            arrive_sum(k).wait()
        energy = tiles[0]
        for k in range(1, count):
            energy += tiles[k]
        energy_ref[...] = energy

        ext = jnp.zeros((ext_rows, width), F32)
        for j in range(match):
            ext += g_ref[:, j : j + 1] * lines[j : j + 1, :]
        for j in range(match):
            row = total - match + j
            ext += g_ref[:, match + j : match + j + 1] * lines[row : row + 1, :]
        lines[total:, :] = ext

        def forward(group, _):
            at = pl.multiple_of(group * GROUP, GROUP)
            seq = [lines[pl.ds(b * BLOCK + at, GROUP), :] for b in range(in_blocks)]
            seq += [None] * (size - in_blocks)
            out = real_transform(seq)
            spec[0, pl.ds(at, GROUP), :width] = out[0][0]
            spec[0, pl.ds(at, GROUP), width:] = out[size // 2][0]
            for f in range(1, size // 2):
                spec[f, pl.ds(at, GROUP), :width] = out[f][0]
                spec[f, pl.ds(at, GROUP), width:] = out[f][1]
            return 0

        lax.fori_loop(0, BLOCK // GROUP, forward, 0)

        def product(f, rights):
            acc = None
            for p in range(PARTS - 1, -1, -1):
                reach = PARTS - p
                got = jnp.dot(
                    t_ref[f, : reach * BLOCK, :], rights[p], preferred_element_type=F32
                )
                for q in range(reach - 1, -1, -1):
                    piece = got[q * BLOCK : (q + 1) * BLOCK]
                    acc = piece if acc is None else acc + piece
            spec[f] = acc

        def halves(f):
            return split_parts(spec[f, :, :width], PARTS), split_parts(spec[f, :, width:], PARTS)

        res, ims = halves(0)
        none = jnp.zeros((BLOCK, width), BF)
        product(
            0,
            [
                jnp.concatenate(
                    [jnp.concatenate([r, none], 1), jnp.concatenate([none, i], 1)], 0
                )
                for r, i in zip(res, ims)
            ],
        )

        def multiply(f, _):
            res, ims = halves(f)
            product(
                f,
                [
                    jnp.concatenate(
                        [jnp.concatenate([r, i], 1), jnp.concatenate([-i, r], 1)], 0
                    )
                    for r, i in zip(res, ims)
                ],
            )
            return 0

        lax.fori_loop(1, size // 2, multiply, 0)

        def backward(group, _):
            at = pl.multiple_of(group * GROUP, GROUP)
            values = [(spec[0, pl.ds(at, GROUP), :width], None)]
            for f in range(1, size // 2):
                values.append(
                    (spec[f, pl.ds(at, GROUP), :width], spec[f, pl.ds(at, GROUP), width:])
                )
            values.append((spec[0, pl.ds(at, GROUP), width:], None))
            for b, value in enumerate(real_inverse(values, size, out_blocks)):
                lines[pl.ds(b * BLOCK + at, GROUP), :] = value
            return 0

        lax.fori_loop(0, BLOCK // GROUP, backward, 0)

        for k in range(count):
            leave(k).start()
        for k in range(count):
            leave(k).wait()

    hbm = pl.BlockSpec(memory_space=pl.ANY)
    vmem = pl.BlockSpec(memory_space=pltpu.VMEM)
    result = pl.pallas_call(
        body,
        name="line_slopes",
        in_specs=[pl.BlockSpec(memory_space=pltpu.SMEM), vmem, vmem] + [hbm] * count,
        out_specs=[hbm] * count + [vmem],
        out_shape=[jax.ShapeDtypeStruct((rows, width), F32)] * count
        + [jax.ShapeDtypeStruct((8, width), F32)],
        scratch_shapes=[
            pltpu.VMEM((in_blocks * BLOCK, width), F32),
            pltpu.VMEM((size // 2, BLOCK, 2 * width), F32),
            pltpu.VMEM((count, 8, width), F32),
            pltpu.SemaphoreType.DMA((count,)),
            pltpu.SemaphoreType.DMA((count,)),
            pltpu.SemaphoreType.DMA((count,)),
        ],
        cost_estimate=pl.CostEstimate(
            flops=12 * size * BLOCK * BLOCK * width,
            bytes_accessed=8 * total * width,
            transcendentals=0,
        ),
    )(place, gram, tables, *pieces)
    return result[:count], result[count]


def advect(velocity, pieces, place, rate):
    rows, lines = velocity.shape
    count = len(pieces)
    width = lines // count
    steps = 8
    chunk = rows // steps

    def body(place_ref, rate_ref, v_ref, *refs):
        ins, (s_ref, f_ref) = refs[:count], refs[count:]
        for k in range(count):
            lane = pl.multiple_of(lax.rem(place_ref[0] + count - k, count) * width, LANE)
            slope = ins[k][...]
            field = v_ref[:, pl.ds(lane, width)]
            s_ref[:, pl.ds(lane, width)] = slope
            f_ref[:, pl.ds(lane, width)] = field - rate_ref[0, 0] * field * slope

    whole = pl.BlockSpec((chunk, lines), lambda i: (i, 0))
    return pl.pallas_call(
        body,
        name="advect",
        grid=(steps,),
        in_specs=[
            pl.BlockSpec(memory_space=pltpu.SMEM),
            pl.BlockSpec(memory_space=pltpu.SMEM),
            whole,
        ]
        + [pl.BlockSpec((chunk, width), lambda i: (i, 0))] * count,
        out_specs=[whole, whole],
        out_shape=[jax.ShapeDtypeStruct((rows, lines), F32)] * 2,
        cost_estimate=pl.CostEstimate(
            flops=rows * lines * 3, bytes_accessed=rows * lines * 16, transcendentals=0
        ),
    )(place, rate, velocity, *pieces)


def exchange(pieces, axis):
    count = len(pieces)
    out = [pieces[0]]
    for k in range(1, count):
        out.append(lax.ppermute(pieces[k], axis, [(i, (i + k) % count) for i in range(count)]))
    return out


def total_over(part, axis):
    size = lax.axis_size(axis)
    moving = part
    for _ in range(size - 1):
        moving = lax.ppermute(moving, axis, [(i, (i + 1) % size) for i in range(size)])
        part = part + moving
    return part


def per_device(velocity, left_gram, right_gram):
    row_count, line_total = velocity.shape
    cont, match = left_gram.shape
    gx_count = lax.axis_size("gx")
    ga_count = lax.axis_size("ga")
    place = lax.axis_index("gx").astype(jnp.int32).reshape(1)
    total = row_count * gx_count
    out_blocks = total // BLOCK
    in_blocks = -(-(total + cont) // BLOCK)
    size = transform_size(out_blocks + in_blocks - 1)

    owned = exchange(pack(velocity, place, gx_count), "gx")
    spectrum = slope_spectrum(total + cont, out_blocks, in_blocks, size)
    tables = toeplitz_tables(jnp.asarray(spectrum))
    gram = jnp.concatenate([left_gram, right_gram], axis=1)
    gram = jnp.pad(gram, ((0, in_blocks * BLOCK - total - cont), (0, 0)))
    slopes, energy = line_slopes(owned, place, gram, tables, cont, match)
    energy = total_over(energy, "ga")
    mean_square = jnp.sum(energy) / (row_count * line_total * gx_count * ga_count)
    advect_rate = (courant / jnp.sqrt(mean_square + epsilon)).reshape(1, 1)
    returned = exchange(slopes, "gx")
    return tuple(advect(velocity, returned, place, advect_rate))


def solution(mesh):
    return jax.shard_map(
        per_device,
        mesh=mesh,
        in_specs=(P("gx", "ga"), P(), P()),
        out_specs=(P("gx", "ga"), P("gx", "ga")),
        check_vma=False,
    )
```

```python
import math

import jax
import jax.numpy as jnp
import numpy as np
from jax import lax
from jax.experimental import pallas as pl
from jax.experimental.pallas import tpu as pltpu
from jax.sharding import PartitionSpec as P

courant = 0.5
epsilon = 1e-06
LANE = 128
GROUP = 8
BF = jnp.bfloat16
F32 = jnp.float32


def add(a, b):
    return b if a is None else a if b is None else a + b


def sub(a, b):
    return a if b is None else -b if a is None else a - b


def scale(a, c):
    return None if a is None else a * np.float32(c)


def turn(value, angle):
    c, s = math.cos(angle), math.sin(angle)
    re, im = value
    return (sub(scale(re, c), scale(im, s)), add(scale(im, c), scale(re, s)))


def real_transform(seq):
    size = len(seq)
    if size == 1:
        return [(seq[0], None)]
    if size == 3:
        far = add(seq[1], seq[2])
        gap = sub(seq[1], seq[2])
        return [
            (add(seq[0], far), None),
            (sub(seq[0], scale(far, 0.5)), scale(gap, -math.sqrt(0.75))),
        ]
    even = real_transform(seq[0::2])
    odd = real_transform(seq[1::2])
    out = [None] * (size // 2 + 1)
    for f in range((size + 3) // 4):
        e = even[f]
        o = odd[f] if f == 0 else turn(odd[f], -2.0 * math.pi * f / size)
        out[f] = (add(e[0], o[0]), add(e[1], o[1]))
        out[size // 2 - f] = (sub(e[0], o[0]), sub(o[1], e[1]))
    if size % 4 == 0:
        f = size // 4
        out[f] = (even[f][0], scale(odd[f][0], -1.0))
    return out


def real_inverse(spec, size, count):
    if count <= 0:
        return []
    if size == 1:
        return [spec[0][0]]
    if size == 3:
        out = [add(spec[0][0], spec[1][0])]
        if count > 1:
            base = sub(spec[0][0], scale(spec[1][0], 0.5))
            side = scale(spec[1][1], math.sqrt(0.75))
            out.append(sub(base, side))
            out.append(add(base, side))
        return out[:count]
    half = size // 2
    even = [None] * (half // 2 + 1)
    odd = [None] * (half // 2 + 1)
    for f in range((size + 3) // 4):
        a, b = spec[f], spec[half - f]
        even[f] = (add(a[0], b[0]), sub(a[1], b[1]))
        diff = (sub(a[0], b[0]), add(a[1], b[1]))
        odd[f] = diff if f == 0 else turn(diff, 2.0 * math.pi * f / size)
    if size % 4 == 0:
        f = size // 4
        even[f] = (spec[f][0], None)
        odd[f] = (scale(spec[f][1], -1.0), None)
    first = real_inverse(even, half, (count + 1) // 2)
    second = real_inverse(odd, half, count // 2)
    out = [None] * count
    out[0::2] = first
    out[1::2] = second
    return out


def transform_size(least):
    size = 1
    while True:
        if size >= least:
            return size
        if size % 2 == 0 and size // 2 * 3 >= least:
            return size // 2 * 3
        size *= 2


def slope_spectrum(period, block, out_blocks, size):
    offsets = np.arange(size)
    offsets = np.where(offsets < out_blocks, offsets, offsets - size)
    step = np.arange(2 * block)
    index = block * offsets[:, None] + block - step[None, :]
    wrapped = (index + period // 2) % period - period // 2
    safe = np.where(wrapped == 0, 1, wrapped)
    sign = np.where(safe % 2 == 0, 1.0, -1.0)
    values = sign * (math.pi / period) / np.sin(math.pi * safe / period)
    values = np.where(wrapped == 0, 0.0, values)
    spectrum = np.fft.fft(values, axis=0)[: size // 2 + 1] / size
    table = np.empty((size, 2 * block))
    table[0] = spectrum[0].real
    table[1] = spectrum[size // 2].real
    table[2::2] = 2.0 * spectrum[1 : size // 2].real
    table[3::2] = 2.0 * spectrum[1 : size // 2].imag
    return table.astype(np.float32)


def split_parts(value):
    high = value.astype(BF)
    rest = value - high.astype(F32)
    mid = rest.astype(BF)
    return high, mid, (rest - mid.astype(F32)).astype(BF)


def left_lanes(shape):
    return lax.broadcasted_iota(jnp.int32, shape, len(shape) - 1) < shape[-1] // 2


def swap(value):
    return pltpu.roll(value, value.shape[-1] // 2, value.ndim - 1)


def merge(left, right):
    return jnp.where(left_lanes(left.shape), left, right)


def toeplitz_tables(spectrum, block):
    slots = spectrum.shape[0] // 2

    def body(w_ref, o_ref):
        def fill(f, _):
            for side in range(2):
                lane = w_ref[pl.ds(2 * f + side, 1), :]
                rows = jnp.broadcast_to(lane, (block, 2 * block))
                rows = pltpu.roll(rows, 0, 1, stride=1, stride_axis=0)[:, block:]
                high, mid, low = split_parts(rows)
                for p, part in enumerate((mid, high, low)):
                    o_ref[f, p * block : (p + 1) * block, side * block : (side + 1) * block] = part
            return 0

        lax.fori_loop(0, slots, fill, 0)

    return pl.pallas_call(
        body,
        name="toeplitz_tables",
        out_shape=jax.ShapeDtypeStruct((slots, 3 * block, 2 * block), BF),
        cost_estimate=pl.CostEstimate(
            flops=slots * block * block * 32,
            bytes_accessed=slots * 3 * block * block * 4,
            transcendentals=0,
        ),
    )(spectrum)


def far_copies(count, place, stacked, pieces, sem, outward):
    rows = stacked.shape[1]
    out = []
    for k in range(count):
        other = lax.rem(place + (k if outward else count - k), count)
        mine = stacked.at[other]
        piece = pieces[k].at[pl.ds(0, rows)]
        pair = (mine, piece) if outward else (piece, mine)
        out.append(pltpu.make_async_copy(pair[0], pair[1], sem.at[k]))
    return out


def run_copies(copies):
    for copy in copies:
        copy.start()
    for copy in copies:
        copy.wait()


ANY = pl.BlockSpec(memory_space=pl.ANY)
SMEM = pl.BlockSpec(memory_space=pltpu.SMEM)
VMEM = pl.BlockSpec(memory_space=pltpu.VMEM)


def pack(view, chunk, count, place, carried):
    per, _, half, lines = view.shape
    span = lines // 2
    width = span // count * 2
    quarter = half // 2
    parts = carried is not None

    def body(place_ref, v_ref, *refs):
        if parts:
            before, outs, packed, sums, sem, sum_sem = refs[0], refs[1:-4], *refs[-4:]
        else:
            packed, sums = refs
        first = jnp.logical_and(pl.program_id(0) == 0, pl.program_id(1) == 0)

        @pl.when(first)
        def _():
            sums[...] = before[...] if parts else jnp.zeros_like(sums)

        if parts:
            at = pl.multiple_of(pl.program_id(0) * half + pl.program_id(1) * quarter, 8)
            rows = pl.ds(at, quarter)
        else:
            rows = slice(None)
        total = sums[...]
        for tile in range(count // 2):
            top = v_ref[0, 0, :, tile * width : (tile + 1) * width]
            low = v_ref[0, 1, :, tile * width : (tile + 1) * width]
            packed[2 * tile, rows, :] = merge(top, swap(low))
            packed[2 * tile + 1, rows, :] = merge(swap(top), low)
            square = top * top + low * low
            total += jnp.sum(square.reshape(quarter // 8, 8, width), axis=0)
        sums[...] = total

        if parts:
            last = jnp.logical_and(pl.program_id(0) == per - 1, pl.program_id(1) == 1)

            @pl.when(last)
            def _():
                copies = far_copies(count, place_ref[0], packed, outs, sem, True)
                for k in range(count):
                    below = outs[k].at[pl.ds(per * half, 8)]
                    copies.append(pltpu.make_async_copy(sums, below, sum_sem.at[k]))
                run_copies(copies)

    in_specs = [SMEM, pl.BlockSpec((1, 2, quarter, span), lambda b, j: (b, 0, j, chunk))]
    cost = pl.CostEstimate(
        flops=per * half * lines * 2, bytes_accessed=per * half * lines * 8, transcendentals=0
    )
    if parts:
        return pl.pallas_call(
            body,
            name="pack_pieces",
            grid=(per, 2),
            in_specs=in_specs + [pl.BlockSpec((8, width), lambda b, j: (0, 0))],
            out_specs=[ANY] * count,
            out_shape=[jax.ShapeDtypeStruct((per * half + 8, width), F32)] * count,
            scratch_shapes=[
                pltpu.VMEM((count, per * half, width), F32),
                pltpu.VMEM((8, width), F32),
                pltpu.SemaphoreType.DMA((count,)),
                pltpu.SemaphoreType.DMA((count,)),
            ],
            cost_estimate=cost,
        )(place, view, carried)
    return pl.pallas_call(
        body,
        name="pack_stacked",
        grid=(per, 2),
        in_specs=in_specs,
        out_specs=[
            pl.BlockSpec((count, quarter, width), lambda b, j: (0, 2 * b + j, 0)),
            pl.BlockSpec((8, width), lambda b, j: (0, 0)),
        ],
        out_shape=[
            jax.ShapeDtypeStruct((count, per * half, width), F32),
            jax.ShapeDtypeStruct((8, width), F32),
        ],
        cost_estimate=cost,
    )(place, view)


def line_slopes(arrived, place, gram, tables, match, spread):
    gather = isinstance(arrived, list)
    count = len(arrived) if gather else arrived.shape[0]
    depth = arrived[0].shape[0] - 8 if gather else arrived.shape[1]
    width = arrived[0].shape[-1]
    slots, block = tables.shape[0], tables.shape[2] // 2
    half = block // 2
    per = depth // half
    out_blocks = per * count
    size = 2 * slots
    ext_rows = gram.shape[0]

    def body(place_ref, g_ref, t_ref, *refs):
        refs = list(refs)
        ins = [refs.pop(0) for _ in range(count if gather else 1)]
        outs = [refs.pop(0) for _ in range(count if spread else 1)]
        if gather:
            energy_ref, lines, tiles, in_sem, sum_sem = [refs.pop(0)] + refs[-4:]
            copies = far_copies(count, place_ref[0], lines, ins, in_sem, False)
            for k in range(count):
                copies.append(
                    pltpu.make_async_copy(
                        ins[k].at[pl.ds(depth, 8)], tiles.at[k], sum_sem.at[k]
                    )
                )
            run_copies(copies)
            energy = tiles[0]
            for k in range(1, count):
                energy += tiles[k]
            energy_ref[...] = energy
        else:
            lines = ins[0]
        spec, extra = refs[:2]
        result = refs[2] if spread else outs[0]

        def at_block(b, at):
            return b // per, pl.ds((b % per) * half + at, GROUP), slice(None)

        ext = jnp.zeros((ext_rows, width), F32)
        for j in range(match):
            ext += g_ref[:, j : j + 1] * lines[0, j : j + 1, :]
        for j in range(match):
            row = depth - match + j
            tail = swap(lines[count - 1, row : row + 1, :])
            ext += g_ref[:, match + j : match + j + 1] * tail
        extra[...] = jnp.zeros_like(extra)
        extra[:ext_rows, :] = merge(ext, jnp.zeros_like(ext))

        def forward(group, _):
            at = pl.multiple_of(group * GROUP, GROUP)
            seq = [lines[at_block(b, at)] for b in range(out_blocks)]
            seq.append(extra[pl.ds(at, GROUP), :])
            out = real_transform(seq + [None] * (size - out_blocks - 1))
            spec[0, pl.ds(at, GROUP), :width] = out[0][0]
            spec[0, pl.ds(at, GROUP), width:] = out[slots][0]
            for f in range(1, slots):
                spec[f, pl.ds(at, GROUP), :width] = out[f][0]
                spec[f, pl.ds(at, GROUP), width:] = out[f][1]
            return 0

        lax.fori_loop(0, half // GROUP, forward, 0)

        def product(f, blocks):
            high, mid, low = split_parts(jnp.concatenate(blocks, 0))
            one = jnp.dot(
                t_ref[f, : 2 * block, :],
                jnp.concatenate([high, mid], 1),
                preferred_element_type=F32,
            )
            two = jnp.dot(
                t_ref[f, block:, :],
                jnp.concatenate([low, high], 1),
                preferred_element_type=F32,
            )
            small = one[:block, width:] + (two[:block, :width] + two[block:, width:])
            got = one[block:, :width] + ((one[:block, :width] + one[block:, width:]) + small)
            top, bottom = got[:half], got[half:]
            spec[f, :, :width] = merge(top, swap(bottom))
            spec[f, :, width:] = merge(swap(top), bottom)

        re, im = spec[0, :, :width], spec[0, :, width:]
        none = jnp.zeros_like(re)
        product(
            0, [merge(re, none), merge(swap(re), none), merge(none, swap(im)), merge(none, im)]
        )

        def multiply(f, _):
            re, im = spec[f, :, :width], spec[f, :, width:]
            re_s, im_s = swap(re), swap(im)
            product(f, [merge(re, im_s), merge(re_s, im), merge(-im, re_s), merge(-im_s, re)])
            return 0

        lax.fori_loop(1, slots, multiply, 0)

        def backward(group, _):
            at = pl.multiple_of(group * GROUP, GROUP)
            values = [(spec[0, pl.ds(at, GROUP), :width], None)]
            for f in range(1, slots):
                values.append(
                    (spec[f, pl.ds(at, GROUP), :width], spec[f, pl.ds(at, GROUP), width:])
                )
            values.append((spec[0, pl.ds(at, GROUP), width:], None))
            for b, value in enumerate(real_inverse(values, size, out_blocks)):
                result[at_block(b, at)] = value
            return 0

        lax.fori_loop(0, half // GROUP, backward, 0)
        if spread:
            run_copies(far_copies(count, place_ref[0], result, outs, refs[3], True))

    scratch = [pltpu.VMEM((slots, half, 2 * width), F32), pltpu.VMEM((half, width), F32)]
    if spread:
        scratch += [pltpu.VMEM((count, depth, width), F32), pltpu.SemaphoreType.DMA((count,))]
        out_specs = [ANY] * count
        out_shape = [jax.ShapeDtypeStruct((depth, width), F32)] * count
    else:
        out_specs = [VMEM]
        out_shape = [jax.ShapeDtypeStruct((count, depth, width), F32)]
    if gather:
        scratch += [
            pltpu.VMEM((count, depth, width), F32),
            pltpu.VMEM((count, 8, width), F32),
            pltpu.SemaphoreType.DMA((count,)),
            pltpu.SemaphoreType.DMA((count,)),
        ]
        out_specs = out_specs + [VMEM]
        out_shape = out_shape + [jax.ShapeDtypeStruct((8, width), F32)]
    out = pl.pallas_call(
        body,
        name="line_slopes",
        in_specs=[SMEM, VMEM, VMEM] + ([ANY] * count if gather else [VMEM]),
        out_specs=out_specs,
        out_shape=out_shape,
        scratch_shapes=scratch,
        cost_estimate=pl.CostEstimate(
            flops=16 * size * block * block * width,
            bytes_accessed=8 * count * depth * width,
            transcendentals=0,
        ),
    )(place, gram, tables, *(arrived if gather else [arrived]))
    energy = out[-1] if gather else None
    return (list(out[:count]) if spread else out[0]), energy


def advect(view, chunk, arrived, place, rate, earlier):
    gather = isinstance(arrived, list)
    per, _, half, lines = view.shape
    span = lines // 2
    count = len(arrived) if gather else arrived.shape[0]
    depth, width = per * half, arrived[0].shape[-1]
    quarter = half // 2
    kept = 0 if earlier is None else 2

    def body(place_ref, rate_ref, v_ref, *refs):
        refs = list(refs)[kept:]
        ins = [refs.pop(0) for _ in range(count if gather else 1)]
        s_ref, f_ref = refs[:2]
        if gather:
            stacked, sem = refs[2:]

            @pl.when(jnp.logical_and(pl.program_id(0) == 0, pl.program_id(1) == 0))
            def _():
                run_copies(far_copies(count, place_ref[0], stacked, ins, sem, False))

            at = pl.multiple_of(pl.program_id(0) * half + pl.program_id(1) * quarter, 8)
            rows = pl.ds(at, quarter)
        else:
            stacked, rows = ins[0], slice(None)
        for tile in range(count // 2):
            lanes = slice(tile * width, (tile + 1) * width)
            one = stacked[2 * tile, rows, :]
            two = stacked[2 * tile + 1, rows, :]
            for side, slope in enumerate((merge(one, swap(two)), merge(swap(one), two))):
                field = v_ref[0, side, :, lanes]
                s_ref[0, side, :, lanes] = slope
                f_ref[0, side, :, lanes] = field - rate_ref[0, 0] * field * slope

    tile_spec = pl.BlockSpec((1, 2, quarter, span), lambda b, j: (b, 0, j, chunk))
    if gather:
        in_specs = [ANY] * count
        scratch = [pltpu.VMEM((count, depth, width), F32), pltpu.SemaphoreType.DMA((count,))]
    else:
        in_specs = [pl.BlockSpec((count, quarter, width), lambda b, j: (0, 2 * b + j, 0))]
        scratch = []
    return pl.pallas_call(
        body,
        name="advect",
        grid=(per, 2),
        in_specs=[SMEM, SMEM, tile_spec] + [ANY] * kept + in_specs,
        out_specs=[tile_spec, tile_spec],
        out_shape=[jax.ShapeDtypeStruct(view.shape, F32)] * 2,
        scratch_shapes=scratch,
        input_output_aliases={3: 0, 4: 1} if kept else {},
        cost_estimate=pl.CostEstimate(
            flops=depth * lines * 3, bytes_accessed=depth * lines * 16, transcendentals=0
        ),
    )(place, rate, view, *(earlier or ()), *(arrived if gather else [arrived]))


def exchange(pieces, axis):
    if not isinstance(pieces, list):
        return lax.all_to_all(pieces, axis, split_axis=0, concat_axis=0, tiled=True)
    count = len(pieces)
    out = [pieces[0]]
    for k in range(1, count):
        out.append(lax.ppermute(pieces[k], axis, [(i, (i + k) % count) for i in range(count)]))
    return out


def total_over(part, axis):
    size = lax.axis_size(axis)
    moving = part
    for _ in range(size - 1):
        moving = lax.ppermute(moving, axis, [(i, (i + 1) % size) for i in range(size)])
        part = part + moving
    return part


def per_device(velocity, left_gram, right_gram):
    row_count, line_total = velocity.shape
    cont, match = left_gram.shape
    gx_count = lax.axis_size("gx")
    ga_count = lax.axis_size("ga")
    place = lax.axis_index("gx").astype(jnp.int32).reshape(1)
    total = row_count * gx_count
    block = 2 * LANE
    while row_count % block or block > LANE:
        block //= 2
    half = block // 2
    assert cont <= half and match <= half and line_total % (gx_count * LANE) == 0
    out_blocks = total // block
    size = transform_size(2 * out_blocks)
    view = velocity.reshape(row_count // block, 2, half, line_total)

    first, sums = pack(view, 0, gx_count, place, None)
    first = exchange(first, "gx")
    second = exchange(list(pack(view, 1, gx_count, place, sums)), "gx")
    spectrum = slope_spectrum(total + cont, block, out_blocks, size)
    tables = toeplitz_tables(jnp.asarray(spectrum), block)
    gram = jnp.concatenate([left_gram, right_gram], axis=1)
    gram = jnp.pad(gram, ((0, -cont % 8), (0, 0)))
    first, _ = line_slopes(first, place, gram, tables, match, False)
    first = exchange(first, "gx")
    second, energy = line_slopes(second, place, gram, tables, match, True)
    second = exchange(second, "gx")
    energy = total_over(energy, "ga")
    mean_square = jnp.sum(energy) / (row_count * line_total * gx_count * ga_count)
    advect_rate = (courant / jnp.sqrt(mean_square + epsilon)).reshape(1, 1)
    done = advect(view, 0, first, place, advect_rate, None)
    done = advect(view, 1, second, place, advect_rate, done)
    return tuple(part.reshape(row_count, line_total) for part in done)


def solution(mesh):
    return jax.shard_map(
        per_device,
        mesh=mesh,
        in_specs=(P("gx", "ga"), P(), P()),
        out_specs=(P("gx", "ga"), P("gx", "ga")),
        check_vma=False,
    )
```

```python
import math

import jax
import jax.numpy as jnp
import numpy as np
from jax import lax
from jax.experimental import pallas as pl
from jax.experimental.pallas import tpu as pltpu
from jax.sharding import PartitionSpec as P

courant = 0.5
epsilon = 1e-06
LANE = 128
GROUP = 8
BF = jnp.bfloat16
F32 = jnp.float32


def add(a, b):
    return b if a is None else a if b is None else a + b


def sub(a, b):
    return a if b is None else -b if a is None else a - b


def scale(a, c):
    return None if a is None else a * np.float32(c)


def turn(value, angle):
    c, s = math.cos(angle), math.sin(angle)
    re, im = value
    return (sub(scale(re, c), scale(im, s)), add(scale(im, c), scale(re, s)))


def real_transform(seq):
    size = len(seq)
    if size == 1:
        return [(seq[0], None)]
    if size == 3:
        far = add(seq[1], seq[2])
        gap = sub(seq[1], seq[2])
        return [
            (add(seq[0], far), None),
            (sub(seq[0], scale(far, 0.5)), scale(gap, -math.sqrt(0.75))),
        ]
    even = real_transform(seq[0::2])
    odd = real_transform(seq[1::2])
    out = [None] * (size // 2 + 1)
    for f in range((size + 3) // 4):
        e = even[f]
        o = odd[f] if f == 0 else turn(odd[f], -2.0 * math.pi * f / size)
        out[f] = (add(e[0], o[0]), add(e[1], o[1]))
        out[size // 2 - f] = (sub(e[0], o[0]), sub(o[1], e[1]))
    if size % 4 == 0:
        f = size // 4
        out[f] = (even[f][0], scale(odd[f][0], -1.0))
    return out


def real_inverse(spec, size, count):
    if count <= 0:
        return []
    if size == 1:
        return [spec[0][0]]
    if size == 3:
        out = [add(spec[0][0], spec[1][0])]
        if count > 1:
            base = sub(spec[0][0], scale(spec[1][0], 0.5))
            side = scale(spec[1][1], math.sqrt(0.75))
            out.append(sub(base, side))
            out.append(add(base, side))
        return out[:count]
    half = size // 2
    even = [None] * (half // 2 + 1)
    odd = [None] * (half // 2 + 1)
    for f in range((size + 3) // 4):
        a, b = spec[f], spec[half - f]
        even[f] = (add(a[0], b[0]), sub(a[1], b[1]))
        diff = (sub(a[0], b[0]), add(a[1], b[1]))
        odd[f] = diff if f == 0 else turn(diff, 2.0 * math.pi * f / size)
    if size % 4 == 0:
        f = size // 4
        even[f] = (spec[f][0], None)
        odd[f] = (scale(spec[f][1], -1.0), None)
    first = real_inverse(even, half, (count + 1) // 2)
    second = real_inverse(odd, half, count // 2)
    out = [None] * count
    out[0::2] = first
    out[1::2] = second
    return out


def transform_size(least):
    size = 1
    while True:
        if size >= least:
            return size
        if size % 2 == 0 and size // 2 * 3 >= least:
            return size // 2 * 3
        size *= 2


def slope_spectrum(period, block, out_blocks, size):
    offsets = np.arange(size)
    offsets = np.where(offsets < out_blocks, offsets, offsets - size)
    step = np.arange(2 * block)
    index = block * offsets[:, None] + block - step[None, :]
    wrapped = (index + period // 2) % period - period // 2
    safe = np.where(wrapped == 0, 1, wrapped)
    sign = np.where(safe % 2 == 0, 1.0, -1.0)
    values = sign * (math.pi / period) / np.sin(math.pi * safe / period)
    values = np.where(wrapped == 0, 0.0, values)
    spectrum = np.fft.fft(values, axis=0)[: size // 2 + 1] / size
    table = np.empty((size, 2 * block))
    table[0] = spectrum[0].real
    table[1] = spectrum[size // 2].real
    table[2::2] = 2.0 * spectrum[1 : size // 2].real
    table[3::2] = 2.0 * spectrum[1 : size // 2].imag
    return table.astype(np.float32)


def split_parts(value):
    high = value.astype(BF)
    rest = value - high.astype(F32)
    mid = rest.astype(BF)
    return high, mid, (rest - mid.astype(F32)).astype(BF)


def left_lanes(shape):
    return lax.broadcasted_iota(jnp.int32, shape, len(shape) - 1) < shape[-1] // 2


def swap(value):
    return pltpu.roll(value, value.shape[-1] // 2, value.ndim - 1)


def merge(left, right):
    return jnp.where(left_lanes(left.shape), left, right)


def toeplitz_tables(spectrum, block):
    slots = spectrum.shape[0] // 2

    def body(w_ref, o_ref):
        def fill(f, _):
            for side in range(2):
                lane = w_ref[pl.ds(2 * f + side, 1), :]
                rows = jnp.broadcast_to(lane, (block, 2 * block))
                rows = pltpu.roll(rows, 0, 1, stride=1, stride_axis=0)[:, block:]
                high, mid, low = split_parts(rows)
                for p, part in enumerate((mid, high, low)):
                    o_ref[f, p * block : (p + 1) * block, side * block : (side + 1) * block] = part
            return 0

        lax.fori_loop(0, slots, fill, 0)

    return pl.pallas_call(
        body,
        name="toeplitz_tables",
        out_shape=jax.ShapeDtypeStruct((slots, 3 * block, 2 * block), BF),
        compiler_params=pltpu.CompilerParams(vmem_limit_bytes=16 << 20),
        cost_estimate=pl.CostEstimate(
            flops=slots * block * block * 32,
            bytes_accessed=slots * 3 * block * block * 4,
            transcendentals=0,
        ),
    )(spectrum)


def far_copies(count, place, stacked, pieces, sem, outward):
    rows = stacked.shape[1]
    out = []
    for k in range(count):
        other = lax.rem(place + (k if outward else count - k), count)
        mine = stacked.at[other]
        piece = pieces[k].at[pl.ds(0, rows)]
        pair = (mine, piece) if outward else (piece, mine)
        out.append(pltpu.make_async_copy(pair[0], pair[1], sem.at[k]))
    return out


def run_copies(copies):
    for copy in copies:
        copy.start()
    for copy in copies:
        copy.wait()


ANY = pl.BlockSpec(memory_space=pl.ANY)
SMEM = pl.BlockSpec(memory_space=pltpu.SMEM)
VMEM = pl.BlockSpec(memory_space=pltpu.VMEM)


def pack(view, chunk, count, place, carried):
    per, _, half, lines = view.shape
    span = lines // 2
    width = span // count * 2
    depth = per * half
    quarter = half // 2
    steps = [(b, q * quarter) for b in range(per) for q in range(2)]
    parts = carried is not None

    def body(place_ref, v_ref, *refs):
        refs = list(refs)
        total = refs.pop(0)[...] if parts else jnp.zeros((8, width), F32)
        outs = [refs.pop(0) for _ in range(count if parts else 1)]
        sums, buf, packed, in_sem, out_sem, sum_sem = refs
        arrive = [
            pltpu.make_async_copy(
                v_ref.at[b, :, pl.ds(r, quarter), pl.ds(chunk * span, span)],
                buf.at[j],
                in_sem.at[j],
            )
            for j, (b, r) in enumerate(steps)
        ]
        for copy in arrive:
            copy.start()
        leave = []
        for j, (b, r) in enumerate(steps):
            arrive[j].wait()
            rows = pl.ds(b * half + r, quarter)
            for tile in range(count // 2):
                top = buf[j, 0, :, tile * width : (tile + 1) * width]
                low = buf[j, 1, :, tile * width : (tile + 1) * width]
                packed[2 * tile, rows, :] = merge(top, swap(low))
                packed[2 * tile + 1, rows, :] = merge(swap(top), low)
                square = top * top + low * low
                total += jnp.sum(square.reshape(quarter // 8, 8, width), axis=0)
            if not parts:
                leave.append(
                    pltpu.make_async_copy(packed.at[:, rows], outs[0].at[:, rows], out_sem.at[j])
                )
                leave[-1].start()
        sums[...] = total
        if parts:
            leave = far_copies(count, place_ref[0], packed, outs, out_sem, True)
            for k in range(count):
                below = outs[k].at[pl.ds(depth, 8)]
                leave.append(pltpu.make_async_copy(sums, below, sum_sem.at[k]))
            for copy in leave:
                copy.start()
        for copy in leave:
            copy.wait()

    if parts:
        outs = [jax.ShapeDtypeStruct((depth + 8, width), F32)] * count
    else:
        outs = [jax.ShapeDtypeStruct((count, depth, width), F32)]
    result = pl.pallas_call(
        body,
        name="pack_pieces" if parts else "pack_stacked",
        in_specs=[SMEM, ANY] + [VMEM] * parts,
        out_specs=[ANY] * len(outs) + [VMEM],
        out_shape=outs + [jax.ShapeDtypeStruct((8, width), F32)],
        scratch_shapes=[
            pltpu.VMEM((len(steps), 2, quarter, span), F32),
            pltpu.VMEM((count, depth, width), F32),
            pltpu.SemaphoreType.DMA((len(steps),)),
            pltpu.SemaphoreType.DMA((max(count, len(steps)),)),
            pltpu.SemaphoreType.DMA((count,)),
        ],
        compiler_params=pltpu.CompilerParams(vmem_limit_bytes=8 << 20),
        cost_estimate=pl.CostEstimate(
            flops=depth * lines * 2, bytes_accessed=depth * lines * 8, transcendentals=0
        ),
    )(place, view, *([carried] if parts else []))
    return (list(result[:count]) if parts else result[0]), result[-1]


def line_slopes(arrived, place, gram, tables, match, spread):
    gather = isinstance(arrived, list)
    count = len(arrived) if gather else arrived.shape[0]
    depth = arrived[0].shape[0] - 8 if gather else arrived.shape[1]
    width = arrived[0].shape[-1]
    slots, block = tables.shape[0], tables.shape[2] // 2
    half = block // 2
    per = depth // half
    out_blocks = per * count
    size = 2 * slots
    ext_rows = gram.shape[0]

    def body(place_ref, g_ref, t_ref, *refs):
        refs = list(refs)
        ins = [refs.pop(0) for _ in range(count if gather else 1)]
        outs = [refs.pop(0) for _ in range(count if spread else 1)]
        if gather:
            energy_ref, lines, tiles, in_sem, sum_sem = [refs.pop(0)] + refs[-4:]
            copies = far_copies(count, place_ref[0], lines, ins, in_sem, False)
            for k in range(count):
                copies.append(
                    pltpu.make_async_copy(
                        ins[k].at[pl.ds(depth, 8)], tiles.at[k], sum_sem.at[k]
                    )
                )
            run_copies(copies)
            energy = tiles[0]
            for k in range(1, count):
                energy += tiles[k]
            energy_ref[...] = energy
        else:
            lines = ins[0]
        spec, extra = refs[:2]
        result = refs[2] if spread else outs[0]

        def at_block(b, at):
            return b // per, pl.ds((b % per) * half + at, GROUP), slice(None)

        ext = jnp.zeros((ext_rows, width), F32)
        for j in range(match):
            ext += g_ref[:, j : j + 1] * lines[0, j : j + 1, :]
        for j in range(match):
            row = depth - match + j
            tail = swap(lines[count - 1, row : row + 1, :])
            ext += g_ref[:, match + j : match + j + 1] * tail
        extra[...] = jnp.zeros_like(extra)
        extra[:ext_rows, :] = merge(ext, jnp.zeros_like(ext))

        def forward(group, _):
            at = pl.multiple_of(group * GROUP, GROUP)
            seq = [lines[at_block(b, at)] for b in range(out_blocks)]
            seq.append(extra[pl.ds(at, GROUP), :])
            out = real_transform(seq + [None] * (size - out_blocks - 1))
            spec[0, pl.ds(at, GROUP), :width] = out[0][0]
            spec[0, pl.ds(at, GROUP), width:] = out[slots][0]
            for f in range(1, slots):
                spec[f, pl.ds(at, GROUP), :width] = out[f][0]
                spec[f, pl.ds(at, GROUP), width:] = out[f][1]
            return 0

        lax.fori_loop(0, half // GROUP, forward, 0)

        def product(f, blocks):
            high, mid, low = split_parts(jnp.concatenate(blocks, 0))
            one = jnp.dot(
                t_ref[f, : 2 * block, :],
                jnp.concatenate([high, mid], 1),
                preferred_element_type=F32,
            )
            two = jnp.dot(
                t_ref[f, block:, :],
                jnp.concatenate([low, high], 1),
                preferred_element_type=F32,
            )
            small = one[:block, width:] + (two[:block, :width] + two[block:, width:])
            got = one[block:, :width] + ((one[:block, :width] + one[block:, width:]) + small)
            top, bottom = got[:half], got[half:]
            spec[f, :, :width] = merge(top, swap(bottom))
            spec[f, :, width:] = merge(swap(top), bottom)

        re, im = spec[0, :, :width], spec[0, :, width:]
        none = jnp.zeros_like(re)
        product(
            0, [merge(re, none), merge(swap(re), none), merge(none, swap(im)), merge(none, im)]
        )

        def multiply(f, _):
            re, im = spec[f, :, :width], spec[f, :, width:]
            re_s, im_s = swap(re), swap(im)
            product(f, [merge(re, im_s), merge(re_s, im), merge(-im, re_s), merge(-im_s, re)])
            return 0

        lax.fori_loop(1, slots, multiply, 0, unroll=4)

        def backward(group, _):
            at = pl.multiple_of(group * GROUP, GROUP)
            values = [(spec[0, pl.ds(at, GROUP), :width], None)]
            for f in range(1, slots):
                values.append(
                    (spec[f, pl.ds(at, GROUP), :width], spec[f, pl.ds(at, GROUP), width:])
                )
            values.append((spec[0, pl.ds(at, GROUP), width:], None))
            for b, value in enumerate(real_inverse(values, size, out_blocks)):
                result[at_block(b, at)] = value
            return 0

        lax.fori_loop(0, half // GROUP, backward, 0)
        if spread:
            run_copies(far_copies(count, place_ref[0], result, outs, refs[3], True))

    scratch = [pltpu.VMEM((slots, half, 2 * width), F32), pltpu.VMEM((half, width), F32)]
    if spread:
        scratch += [pltpu.VMEM((count, depth, width), F32), pltpu.SemaphoreType.DMA((count,))]
        out_specs = [ANY] * count
        out_shape = [jax.ShapeDtypeStruct((depth, width), F32)] * count
    else:
        out_specs = [VMEM]
        out_shape = [jax.ShapeDtypeStruct((count, depth, width), F32)]
    if gather:
        scratch += [
            pltpu.VMEM((count, depth, width), F32),
            pltpu.VMEM((count, 8, width), F32),
            pltpu.SemaphoreType.DMA((count,)),
            pltpu.SemaphoreType.DMA((count,)),
        ]
        out_specs = out_specs + [VMEM]
        out_shape = out_shape + [jax.ShapeDtypeStruct((8, width), F32)]
    out = pl.pallas_call(
        body,
        name="line_slopes",
        in_specs=[SMEM, VMEM, VMEM] + ([ANY] * count if gather else [VMEM]),
        out_specs=out_specs,
        out_shape=out_shape,
        scratch_shapes=scratch,
        compiler_params=pltpu.CompilerParams(vmem_limit_bytes=28 << 20),
        cost_estimate=pl.CostEstimate(
            flops=16 * size * block * block * width,
            bytes_accessed=8 * count * depth * width,
            transcendentals=0,
        ),
    )(place, gram, tables, *(arrived if gather else [arrived]))
    energy = out[-1] if gather else None
    return (list(out[:count]) if spread else out[0]), energy


def advect(view, chunk, arrived, place, rate, earlier):
    gather = isinstance(arrived, list)
    per, _, half, lines = view.shape
    span = lines // 2
    count = len(arrived) if gather else arrived.shape[0]
    depth, width = per * half, arrived[0].shape[-1]
    quarter = half // 2
    steps = [(b, q * quarter) for b in range(per) for q in range(2)]
    kept = 0 if earlier is None else 2

    def body(place_ref, rate_ref, v_ref, *refs):
        refs = list(refs)[kept:]
        ins = [refs.pop(0) for _ in range(count if gather else 1)]
        s_ref, f_ref, v_buf, stacked, s_buf, f_buf, v_sem, in_sem, s_sem, f_sem = refs

        def part(ref, j):
            b, r = steps[j]
            return ref.at[b, :, pl.ds(r, quarter), pl.ds(chunk * span, span)]

        fields = [
            pltpu.make_async_copy(part(v_ref, j), v_buf.at[j], v_sem.at[j])
            for j in range(len(steps))
        ]
        if gather:
            pieces = far_copies(count, place_ref[0], stacked, ins, in_sem, False)
        else:
            pieces = [pltpu.make_async_copy(ins[0], stacked, in_sem.at[0])]
        for copy in pieces + fields:
            copy.start()
        for copy in pieces:
            copy.wait()
        rate = rate_ref[0, 0]
        leave = []
        for j, (b, r) in enumerate(steps):
            fields[j].wait()
            rows = pl.ds(b * half + r, quarter)
            for tile in range(count // 2):
                lanes = slice(tile * width, (tile + 1) * width)
                one = stacked[2 * tile, rows, :]
                two = stacked[2 * tile + 1, rows, :]
                for side, slope in enumerate((merge(one, swap(two)), merge(swap(one), two))):
                    field = v_buf[j, side, :, lanes]
                    s_buf[j, side, :, lanes] = slope
                    f_buf[j, side, :, lanes] = field - rate * field * slope
            leave.append(pltpu.make_async_copy(s_buf.at[j], part(s_ref, j), s_sem.at[j]))
            leave.append(pltpu.make_async_copy(f_buf.at[j], part(f_ref, j), f_sem.at[j]))
            leave[-2].start()
            leave[-1].start()
        for copy in leave:
            copy.wait()

    tiles = pltpu.VMEM((len(steps), 2, quarter, span), F32)
    step_sem = pltpu.SemaphoreType.DMA((len(steps),))
    return pl.pallas_call(
        body,
        name="advect",
        in_specs=[SMEM, SMEM, ANY] + [ANY] * kept + [ANY] * (count if gather else 1),
        out_specs=[ANY, ANY],
        out_shape=[jax.ShapeDtypeStruct(view.shape, F32)] * 2,
        scratch_shapes=[
            tiles,
            pltpu.VMEM((count, depth, width), F32),
            tiles,
            tiles,
            step_sem,
            pltpu.SemaphoreType.DMA((count,)),
            step_sem,
            step_sem,
        ],
        input_output_aliases={3: 0, 4: 1} if kept else {},
        compiler_params=pltpu.CompilerParams(vmem_limit_bytes=12 << 20),
        cost_estimate=pl.CostEstimate(
            flops=depth * lines * 3, bytes_accessed=depth * lines * 16, transcendentals=0
        ),
    )(place, rate, view, *(earlier or ()), *(arrived if gather else [arrived]))


def exchange(pieces, axis):
    if not isinstance(pieces, list):
        return lax.all_to_all(pieces, axis, split_axis=0, concat_axis=0, tiled=True)
    count = len(pieces)
    out = [pieces[0]]
    for k in range(1, count):
        moved = lax.ppermute(pieces[k], axis, [(i, (i + k) % count) for i in range(count)])
        out.append(moved)
    return out


def total_over(part, axis):
    size = lax.axis_size(axis)
    moving = part
    for _ in range(size - 1):
        moving = lax.ppermute(moving, axis, [(i, (i + 1) % size) for i in range(size)])
        part = part + moving
    return part


def per_device(velocity, left_gram, right_gram):
    row_count, line_total = velocity.shape
    cont, match = left_gram.shape
    gx_count = lax.axis_size("gx")
    ga_count = lax.axis_size("ga")
    place = lax.axis_index("gx").astype(jnp.int32).reshape(1)
    total = row_count * gx_count
    block = 2 * LANE
    while row_count % block or block > LANE:
        block //= 2
    half = block // 2
    assert cont <= half and match <= half and line_total % (gx_count * LANE) == 0
    out_blocks = total // block
    size = transform_size(2 * out_blocks)
    view = velocity.reshape(row_count // block, 2, half, line_total)

    first, sums = pack(view, 0, gx_count, place, None)
    first = exchange(first, "gx")
    second, _ = pack(view, 1, gx_count, place, sums)
    second = exchange(second, "gx")
    spectrum = slope_spectrum(total + cont, block, out_blocks, size)
    tables = toeplitz_tables(jnp.asarray(spectrum), block)
    gram = jnp.concatenate([left_gram, right_gram], axis=1)
    gram = jnp.pad(gram, ((0, -cont % 8), (0, 0)))
    first, _ = line_slopes(first, place, gram, tables, match, False)
    first = exchange(first, "gx")
    second, energy = line_slopes(second, place, gram, tables, match, True)
    second = exchange(second, "gx")
    energy = total_over(energy, "ga")
    mean_square = jnp.sum(energy) / (row_count * line_total * gx_count * ga_count)
    advect_rate = (courant / jnp.sqrt(mean_square + epsilon)).reshape(1, 1)
    done = advect(view, 0, first, place, advect_rate, None)
    done = advect(view, 1, second, place, advect_rate, done)
    return tuple(part.reshape(row_count, line_total) for part in done)


def solution(mesh):
    return jax.shard_map(
        per_device,
        mesh=mesh,
        in_specs=(P("gx", "ga"), P(), P()),
        out_specs=(P("gx", "ga"), P("gx", "ga")),
        check_vma=False,
    )
```

```python
import math

import jax
import jax.numpy as jnp
import numpy as np
from jax import lax
from jax.experimental import pallas as pl
from jax.experimental.pallas import tpu as pltpu
from jax.sharding import PartitionSpec as P

courant = 0.5
epsilon = 1e-06
LANE = 128
GROUP = 8
BF = jnp.bfloat16
F32 = jnp.float32


def add(a, b):
    return b if a is None else a if b is None else a + b


def sub(a, b):
    return a if b is None else -b if a is None else a - b


def scale(a, c):
    return None if a is None else a * np.float32(c)


def turn(value, angle):
    c, s = math.cos(angle), math.sin(angle)
    re, im = value
    return (sub(scale(re, c), scale(im, s)), add(scale(im, c), scale(re, s)))


def real_transform(seq):
    size = len(seq)
    if size == 1:
        return [(seq[0], None)]
    if size == 3:
        far = add(seq[1], seq[2])
        gap = sub(seq[1], seq[2])
        return [
            (add(seq[0], far), None),
            (sub(seq[0], scale(far, 0.5)), scale(gap, -math.sqrt(0.75))),
        ]
    even = real_transform(seq[0::2])
    odd = real_transform(seq[1::2])
    out = [None] * (size // 2 + 1)
    for f in range((size + 3) // 4):
        e = even[f]
        o = odd[f] if f == 0 else turn(odd[f], -2.0 * math.pi * f / size)
        out[f] = (add(e[0], o[0]), add(e[1], o[1]))
        out[size // 2 - f] = (sub(e[0], o[0]), sub(o[1], e[1]))
    if size % 4 == 0:
        f = size // 4
        out[f] = (even[f][0], scale(odd[f][0], -1.0))
    return out


def real_inverse(spec, size, count):
    if count <= 0:
        return []
    if size == 1:
        return [spec[0][0]]
    if size == 3:
        out = [add(spec[0][0], spec[1][0])]
        if count > 1:
            base = sub(spec[0][0], scale(spec[1][0], 0.5))
            side = scale(spec[1][1], math.sqrt(0.75))
            out.append(sub(base, side))
            out.append(add(base, side))
        return out[:count]
    half = size // 2
    even = [None] * (half // 2 + 1)
    odd = [None] * (half // 2 + 1)
    for f in range((size + 3) // 4):
        a, b = spec[f], spec[half - f]
        even[f] = (add(a[0], b[0]), sub(a[1], b[1]))
        diff = (sub(a[0], b[0]), add(a[1], b[1]))
        odd[f] = diff if f == 0 else turn(diff, 2.0 * math.pi * f / size)
    if size % 4 == 0:
        f = size // 4
        even[f] = (spec[f][0], None)
        odd[f] = (scale(spec[f][1], -1.0), None)
    first = real_inverse(even, half, (count + 1) // 2)
    second = real_inverse(odd, half, count // 2)
    out = [None] * count
    out[0::2] = first
    out[1::2] = second
    return out


def transform_size(least):
    size = 1
    while True:
        if size >= least:
            return size
        if size % 2 == 0 and size // 2 * 3 >= least:
            return size // 2 * 3
        size *= 2


def slope_spectrum(period, block, out_blocks, size):
    offsets = np.arange(size)
    offsets = np.where(offsets < out_blocks, offsets, offsets - size)
    step = np.arange(2 * block)
    index = block * offsets[:, None] + block - step[None, :]
    wrapped = (index + period // 2) % period - period // 2
    safe = np.where(wrapped == 0, 1, wrapped)
    sign = np.where(safe % 2 == 0, 1.0, -1.0)
    values = sign * (math.pi / period) / np.sin(math.pi * safe / period)
    values = np.where(wrapped == 0, 0.0, values)
    spectrum = np.fft.fft(values, axis=0)[: size // 2 + 1] / size
    table = np.empty((size, 2 * block))
    table[0] = spectrum[0].real
    table[1] = spectrum[size // 2].real
    table[2::2] = 2.0 * spectrum[1 : size // 2].real
    table[3::2] = 2.0 * spectrum[1 : size // 2].imag
    return table.astype(np.float32)


def split_parts(value):
    high = value.astype(BF)
    rest = value - high.astype(F32)
    mid = rest.astype(BF)
    return high, mid, (rest - mid.astype(F32)).astype(BF)


def left_lanes(shape):
    return lax.broadcasted_iota(jnp.int32, shape, len(shape) - 1) < shape[-1] // 2


def swap(value):
    return pltpu.roll(value, value.shape[-1] // 2, value.ndim - 1)


def merge(left, right):
    return jnp.where(left_lanes(left.shape), left, right)


def toeplitz_tables(spectrum, block):
    slots = spectrum.shape[0] // 2

    def body(w_ref, o_ref):
        def fill(f, _):
            for side in range(2):
                lane = w_ref[pl.ds(2 * f + side, 1), :]
                rows = jnp.broadcast_to(lane, (block, 2 * block))
                rows = pltpu.roll(rows, 0, 1, stride=1, stride_axis=0)[:, block:]
                high, mid, low = split_parts(rows)
                for p, part in enumerate((mid, high, low)):
                    o_ref[f, p * block : (p + 1) * block, side * block : (side + 1) * block] = part
            return 0

        lax.fori_loop(0, slots, fill, 0)

    return pl.pallas_call(
        body,
        name="toeplitz_tables",
        out_shape=jax.ShapeDtypeStruct((slots, 3 * block, 2 * block), BF),
        compiler_params=pltpu.CompilerParams(vmem_limit_bytes=58 << 20),
        cost_estimate=pl.CostEstimate(
            flops=slots * block * block * 32,
            bytes_accessed=slots * 3 * block * block * 4,
            transcendentals=0,
        ),
    )(spectrum)


def far_copies(count, place, stacked, pieces, sem, outward):
    rows = stacked.shape[1]
    out = []
    for k in range(count):
        other = lax.rem(place + (k if outward else count - k), count)
        mine = stacked.at[other]
        piece = pieces[k].at[pl.ds(0, rows)]
        pair = (mine, piece) if outward else (piece, mine)
        out.append(pltpu.make_async_copy(pair[0], pair[1], sem.at[k]))
    return out


def run_copies(copies):
    for copy in copies:
        copy.start()
    for copy in copies:
        copy.wait()


HBM = pl.BlockSpec(memory_space=pltpu.HBM)
SMEM = pl.BlockSpec(memory_space=pltpu.SMEM)
VMEM = pl.BlockSpec(memory_space=pltpu.VMEM)


def pack(view, chunk, count, place, carried, parts):
    per, _, half, lines = view.shape
    span = lines // 2
    width = span // count * 2
    depth = per * half
    quarter = half // 2
    steps = [(b, q * quarter) for b in range(per) for q in range(2)]

    def body(place_ref, v_ref, *refs):
        refs = list(refs)
        total = jnp.zeros((8, width), F32) if carried is None else refs.pop(0)[...]
        outs = [refs.pop(0) for _ in range(count if parts else 1)]
        sums, buf, packed, in_sem, out_sem = refs
        arrive = [
            pltpu.make_async_copy(
                v_ref.at[b, :, pl.ds(r, quarter), pl.ds(chunk * span, span)],
                buf.at[j],
                in_sem.at[j],
            )
            for j, (b, r) in enumerate(steps)
        ]
        for copy in arrive:
            copy.start()
        leave = []
        for j, (b, r) in enumerate(steps):
            arrive[j].wait()
            rows = pl.ds(b * half + r, quarter)
            for tile in range(count // 2):
                top = buf[j, 0, :, tile * width : (tile + 1) * width]
                low = buf[j, 1, :, tile * width : (tile + 1) * width]
                packed[2 * tile, rows, :] = merge(top, swap(low))
                packed[2 * tile + 1, rows, :] = merge(swap(top), low)
                square = top * top + low * low
                total += jnp.sum(square.reshape(quarter // 8, 8, width), axis=0)
            if not parts:
                leave.append(
                    pltpu.make_async_copy(packed.at[:, rows], outs[0].at[:, rows], out_sem.at[j])
                )
                leave[-1].start()
        sums[...] = total
        if parts:
            leave = far_copies(count, place_ref[0], packed, outs, out_sem, True)
            for copy in leave:
                copy.start()
        for copy in leave:
            copy.wait()

    if parts:
        outs = [jax.ShapeDtypeStruct((depth, width), F32)] * count
    else:
        outs = [jax.ShapeDtypeStruct((count, depth, width), F32)]
    result = pl.pallas_call(
        body,
        name="pack_pieces" if parts else "pack_stacked",
        in_specs=[SMEM, HBM] + [VMEM] * (carried is not None),
        out_specs=[HBM] * len(outs) + [VMEM],
        out_shape=outs + [jax.ShapeDtypeStruct((8, width), F32)],
        scratch_shapes=[
            pltpu.VMEM((len(steps), 2, quarter, span), F32),
            pltpu.VMEM((count, depth, width), F32),
            pltpu.SemaphoreType.DMA((len(steps),)),
            pltpu.SemaphoreType.DMA((max(count, len(steps)),)),
        ],
        compiler_params=pltpu.CompilerParams(vmem_limit_bytes=58 << 20),
        cost_estimate=pl.CostEstimate(
            flops=depth * lines * 2, bytes_accessed=depth * lines * 8, transcendentals=0
        ),
    )(place, view, *([] if carried is None else [carried]))
    return (list(result[:count]) if parts else result[0]), result[-1]


def line_slopes(arrived, place, gram, tables, match, sums):
    gather = isinstance(arrived, list)
    spread = sums is not None
    count = len(arrived) if gather else arrived.shape[0]
    depth, width = arrived[0].shape[-2:]
    slots, block = tables.shape[0], tables.shape[2] // 2
    half = block // 2
    per = depth // half
    out_blocks = per * count
    size = 2 * slots
    ext_rows = gram.shape[0]
    cuts = 4
    cut = slots // cuts

    def body(place_ref, g_ref, table_ref, *refs):
        refs = list(refs)
        sums_ref = refs.pop(0) if spread else None
        ins = [refs.pop(0) for _ in range(count if gather else 1)]
        outs = [refs.pop(0) for _ in range(count if spread else 1)]
        t_ref, spec, extra, lines, result, table_sem, in_sem, out_sem, sum_sem = refs
        load = [
            pltpu.make_async_copy(
                table_ref.at[pl.ds(c * cut, cut)], t_ref.at[pl.ds(c * cut, cut)], table_sem.at[c]
            )
            for c in range(cuts)
        ]
        if gather:
            copies = far_copies(count, place_ref[0], lines, ins, in_sem, False)
        else:
            copies = [pltpu.make_async_copy(ins[0], lines, in_sem.at[0])]
        for copy in copies + load:
            copy.start()
        for copy in copies:
            copy.wait()

        def at_block(b, at):
            return b // per, pl.ds((b % per) * half + at, GROUP), slice(None)

        ext = jnp.zeros((ext_rows, width), F32)
        for j in range(match):
            ext += g_ref[:, j : j + 1] * lines[0, j : j + 1, :]
        for j in range(match):
            row = depth - match + j
            tail = swap(lines[count - 1, row : row + 1, :])
            ext += g_ref[:, match + j : match + j + 1] * tail
        extra[...] = jnp.zeros_like(extra)
        extra[:ext_rows, :] = merge(ext, jnp.zeros_like(ext))

        def forward(group, _):
            at = pl.multiple_of(group * GROUP, GROUP)
            seq = [lines[at_block(b, at)] for b in range(out_blocks)]
            seq.append(extra[pl.ds(at, GROUP), :])
            out = real_transform(seq + [None] * (size - out_blocks - 1))
            spec[0, pl.ds(at, GROUP), :width] = out[0][0]
            spec[0, pl.ds(at, GROUP), width:] = out[slots][0]
            for f in range(1, slots):
                spec[f, pl.ds(at, GROUP), :width] = out[f][0]
                spec[f, pl.ds(at, GROUP), width:] = out[f][1]
            return 0

        lax.fori_loop(0, half // GROUP, forward, 0)
        for copy in load:
            copy.wait()

        def product(f, blocks):
            high, mid, low = split_parts(jnp.concatenate(blocks, 0))
            one = jnp.dot(
                t_ref[f, : 2 * block, :],
                jnp.concatenate([high, mid], 1),
                preferred_element_type=F32,
            )
            two = jnp.dot(
                t_ref[f, block:, :],
                jnp.concatenate([low, high], 1),
                preferred_element_type=F32,
            )
            small = one[:block, width:] + (two[:block, :width] + two[block:, width:])
            got = one[block:, :width] + ((one[:block, :width] + one[block:, width:]) + small)
            top, bottom = got[:half], got[half:]
            spec[f, :, :width] = merge(top, swap(bottom))
            spec[f, :, width:] = merge(swap(top), bottom)

        re, im = spec[0, :, :width], spec[0, :, width:]
        none = jnp.zeros_like(re)
        product(
            0, [merge(re, none), merge(swap(re), none), merge(none, swap(im)), merge(none, im)]
        )

        def multiply(f, _):
            re, im = spec[f, :, :width], spec[f, :, width:]
            re_s, im_s = swap(re), swap(im)
            product(f, [merge(re, im_s), merge(re_s, im), merge(-im, re_s), merge(-im_s, re)])
            return 0

        lax.fori_loop(1, slots, multiply, 0, unroll=4)

        def backward(group, _):
            at = pl.multiple_of(group * GROUP, GROUP)
            values = [(spec[0, pl.ds(at, GROUP), :width], None)]
            for f in range(1, slots):
                values.append(
                    (spec[f, pl.ds(at, GROUP), :width], spec[f, pl.ds(at, GROUP), width:])
                )
            values.append((spec[0, pl.ds(at, GROUP), width:], None))
            for b, value in enumerate(real_inverse(values, size, out_blocks)):
                result[at_block(b, at)] = value
            return 0

        lax.fori_loop(0, half // GROUP, backward, 0)
        if spread:
            copies = far_copies(count, place_ref[0], result, outs, out_sem, True)
            for k in range(count):
                below = outs[k].at[pl.ds(depth, 8)]
                copies.append(pltpu.make_async_copy(sums_ref, below, sum_sem.at[k]))
        else:
            copies = [pltpu.make_async_copy(result, outs[0], out_sem.at[0])]
        run_copies(copies)

    if spread:
        out_shape = [jax.ShapeDtypeStruct((depth + 8, width), F32)] * count
    else:
        out_shape = [jax.ShapeDtypeStruct((count, depth, width), F32)]
    stacked = pltpu.VMEM((count, depth, width), F32)
    out = pl.pallas_call(
        body,
        name="line_slopes",
        in_specs=[SMEM, VMEM, HBM] + [VMEM] * spread + [HBM] * (count if gather else 1),
        out_specs=[HBM] * len(out_shape),
        out_shape=out_shape,
        scratch_shapes=[
            pltpu.VMEM(tables.shape, BF),
            pltpu.VMEM((slots, half, 2 * width), F32),
            pltpu.VMEM((half, width), F32),
            stacked,
            stacked,
            pltpu.SemaphoreType.DMA((cuts,)),
            pltpu.SemaphoreType.DMA((count,)),
            pltpu.SemaphoreType.DMA((count,)),
            pltpu.SemaphoreType.DMA((count,)),
        ],
        compiler_params=pltpu.CompilerParams(vmem_limit_bytes=50 << 20),
        cost_estimate=pl.CostEstimate(
            flops=16 * size * block * block * width,
            bytes_accessed=8 * count * depth * width,
            transcendentals=0,
        ),
    )(place, gram, tables, *([sums] if spread else []), *(arrived if gather else [arrived]))
    return list(out) if spread else out[0]


def advect(view, chunk, arrived, place, points, energy, earlier):
    gather = isinstance(arrived, list)
    per, _, half, lines = view.shape
    span = lines // 2
    count = len(arrived) if gather else arrived.shape[0]
    depth, width = per * half, arrived[0].shape[-1]
    quarter = half // 2
    steps = [(b, q * quarter) for b in range(per) for q in range(2)]
    kept = 0 if earlier is None else 2

    def body(place_ref, v_ref, *refs):
        refs = list(refs)[kept:]
        energy_in = None if gather else refs.pop(0)
        ins = [refs.pop(0) for _ in range(count if gather else 1)]
        s_ref, f_ref = refs.pop(0), refs.pop(0)
        energy_out = refs.pop(0) if gather else None
        v_buf, stacked, tiles, s_buf, f_buf, v_sem, in_sem, sum_sem, s_sem, f_sem = refs

        def part(ref, j):
            b, r = steps[j]
            return ref.at[b, :, pl.ds(r, quarter), pl.ds(chunk * span, span)]

        fields = [
            pltpu.make_async_copy(part(v_ref, j), v_buf.at[j], v_sem.at[j])
            for j in range(len(steps))
        ]
        if gather:
            pieces = far_copies(count, place_ref[0], stacked, ins, in_sem, False)
            for k in range(count):
                below = ins[k].at[pl.ds(depth, 8)]
                pieces.append(pltpu.make_async_copy(below, tiles.at[k], sum_sem.at[k]))
        else:
            pieces = [pltpu.make_async_copy(ins[0], stacked, in_sem.at[0])]
        for copy in pieces + fields:
            copy.start()
        for copy in pieces:
            copy.wait()
        if gather:
            tile = tiles[0]
            for k in range(1, count):
                tile += tiles[k]
            energy_out[...] = tile
        else:
            tile = energy_in[...]
        lane_sum = jnp.sum(tile, axis=0, keepdims=True)
        mean_square = jnp.sum(lane_sum, axis=1, keepdims=True) / points
        rate = jnp.broadcast_to(courant / jnp.sqrt(mean_square + epsilon), (quarter, width))
        leave = []
        for j, (b, r) in enumerate(steps):
            fields[j].wait()
            rows = pl.ds(b * half + r, quarter)
            for tile in range(count // 2):
                lanes = slice(tile * width, (tile + 1) * width)
                one = stacked[2 * tile, rows, :]
                two = stacked[2 * tile + 1, rows, :]
                for side, slope in enumerate((merge(one, swap(two)), merge(swap(one), two))):
                    field = v_buf[j, side, :, lanes]
                    s_buf[j, side, :, lanes] = slope
                    f_buf[j, side, :, lanes] = field - rate * field * slope
            leave.append(pltpu.make_async_copy(s_buf.at[j], part(s_ref, j), s_sem.at[j]))
            leave.append(pltpu.make_async_copy(f_buf.at[j], part(f_ref, j), f_sem.at[j]))
            leave[-2].start()
            leave[-1].start()
        for copy in leave:
            copy.wait()

    buffer = pltpu.VMEM((len(steps), 2, quarter, span), F32)
    step_sem = pltpu.SemaphoreType.DMA((len(steps),))
    piece_sem = pltpu.SemaphoreType.DMA((count,))
    out = pl.pallas_call(
        body,
        name="advect",
        in_specs=[SMEM, HBM]
        + [HBM] * kept
        + ([HBM] * count if gather else [VMEM, HBM]),
        out_specs=[HBM, HBM] + [VMEM] * gather,
        out_shape=[jax.ShapeDtypeStruct(view.shape, F32)] * 2
        + [jax.ShapeDtypeStruct((8, width), F32)] * gather,
        scratch_shapes=[
            buffer,
            pltpu.VMEM((count, depth, width), F32),
            pltpu.VMEM((count, 8, width), F32),
            buffer,
            buffer,
            step_sem,
            piece_sem,
            piece_sem,
            step_sem,
            step_sem,
        ],
        input_output_aliases={2: 0, 3: 1} if kept else {},
        compiler_params=pltpu.CompilerParams(vmem_limit_bytes=12 << 20),
        cost_estimate=pl.CostEstimate(
            flops=depth * lines * 3, bytes_accessed=depth * lines * 16, transcendentals=0
        ),
    )(place, view, *(earlier or ()), *(arrived if gather else [energy, arrived]))
    return out[:2], (out[2] if gather else energy)


def exchange(pieces, axis):
    if not isinstance(pieces, list):
        return lax.all_to_all(pieces, axis, split_axis=0, concat_axis=0, tiled=True)
    count = len(pieces)
    out = [pieces[0]]
    for k in range(1, count):
        moved = lax.ppermute(pieces[k], axis, [(i, (i + k) % count) for i in range(count)])
        out.append(moved)
    return out


def total_over(part, axis):
    size = lax.axis_size(axis)
    moving = part
    for _ in range(size - 1):
        moving = lax.ppermute(moving, axis, [(i, (i + 1) % size) for i in range(size)])
        part = part + moving
    return part


def per_device(velocity, left_gram, right_gram):
    row_count, line_total = velocity.shape
    cont, match = left_gram.shape
    gx_count = lax.axis_size("gx")
    ga_count = lax.axis_size("ga")
    place = lax.axis_index("gx").astype(jnp.int32).reshape(1)
    total = row_count * gx_count
    block = 2 * LANE
    while row_count % block or block > LANE:
        block //= 2
    half = block // 2
    assert cont <= half and match <= half and line_total % (gx_count * LANE) == 0
    out_blocks = total // block
    size = transform_size(2 * out_blocks)
    view = velocity.reshape(row_count // block, 2, half, line_total)

    points = row_count * line_total * gx_count * ga_count

    first, sums = pack(view, 0, gx_count, place, None, True)
    first = exchange(first, "gx")
    second, sums = pack(view, 1, gx_count, place, sums, False)
    second = exchange(second, "gx")
    sums = total_over(sums, "ga")
    spectrum = slope_spectrum(total + cont, block, out_blocks, size)
    tables = toeplitz_tables(jnp.asarray(spectrum), block)
    gram = jnp.concatenate([left_gram, right_gram], axis=1)
    gram = jnp.pad(gram, ((0, -cont % 8), (0, 0)))
    first = line_slopes(first, place, gram, tables, match, sums)
    first = exchange(first, "gx")
    second = line_slopes(second, place, gram, tables, match, None)
    second = exchange(second, "gx")
    done, energy = advect(view, 0, first, place, points, None, None)
    done, _ = advect(view, 1, second, place, points, energy, done)
    return tuple(part.reshape(row_count, line_total) for part in done)


def solution(mesh):
    return jax.shard_map(
        per_device,
        mesh=mesh,
        in_specs=(P("gx", "ga"), P(), P()),
        out_specs=(P("gx", "ga"), P("gx", "ga")),
        check_vma=False,
    )
```

```python
import math

import jax
import jax.numpy as jnp
import numpy as np
from jax import lax
from jax.experimental import pallas as pl
from jax.experimental.pallas import tpu as pltpu
from jax.sharding import PartitionSpec as P

courant = 0.5
epsilon = 1e-06
LANE = 128
GROUP = 8
BF = jnp.bfloat16
F32 = jnp.float32


def add(a, b):
    return b if a is None else a if b is None else a + b


def sub(a, b):
    return a if b is None else -b if a is None else a - b


def scale(a, c):
    return None if a is None else a * np.float32(c)


def turn(value, angle):
    c, s = math.cos(angle), math.sin(angle)
    re, im = value
    return (sub(scale(re, c), scale(im, s)), add(scale(im, c), scale(re, s)))


def real_transform(seq):
    size = len(seq)
    if size == 1:
        return [(seq[0], None)]
    if size == 3:
        far = add(seq[1], seq[2])
        gap = sub(seq[1], seq[2])
        return [
            (add(seq[0], far), None),
            (sub(seq[0], scale(far, 0.5)), scale(gap, -math.sqrt(0.75))),
        ]
    even = real_transform(seq[0::2])
    odd = real_transform(seq[1::2])
    out = [None] * (size // 2 + 1)
    for f in range((size + 3) // 4):
        e = even[f]
        o = odd[f] if f == 0 else turn(odd[f], -2.0 * math.pi * f / size)
        out[f] = (add(e[0], o[0]), add(e[1], o[1]))
        out[size // 2 - f] = (sub(e[0], o[0]), sub(o[1], e[1]))
    if size % 4 == 0:
        f = size // 4
        out[f] = (even[f][0], scale(odd[f][0], -1.0))
    return out


def real_inverse(spec, size, count):
    if count <= 0:
        return []
    if size == 1:
        return [spec[0][0]]
    if size == 3:
        out = [add(spec[0][0], spec[1][0])]
        if count > 1:
            base = sub(spec[0][0], scale(spec[1][0], 0.5))
            side = scale(spec[1][1], math.sqrt(0.75))
            out.append(sub(base, side))
            out.append(add(base, side))
        return out[:count]
    half = size // 2
    even = [None] * (half // 2 + 1)
    odd = [None] * (half // 2 + 1)
    for f in range((size + 3) // 4):
        a, b = spec[f], spec[half - f]
        even[f] = (add(a[0], b[0]), sub(a[1], b[1]))
        diff = (sub(a[0], b[0]), add(a[1], b[1]))
        odd[f] = diff if f == 0 else turn(diff, 2.0 * math.pi * f / size)
    if size % 4 == 0:
        f = size // 4
        even[f] = (spec[f][0], None)
        odd[f] = (scale(spec[f][1], -1.0), None)
    first = real_inverse(even, half, (count + 1) // 2)
    second = real_inverse(odd, half, count // 2)
    out = [None] * count
    out[0::2] = first
    out[1::2] = second
    return out


def transform_size(least):
    size = 1
    while True:
        if size >= least:
            return size
        if size % 2 == 0 and size // 2 * 3 >= least:
            return size // 2 * 3
        size *= 2


def slope_spectrum(period, block, out_blocks, size):
    offsets = np.arange(size)
    offsets = np.where(offsets < out_blocks, offsets, offsets - size)
    step = np.arange(2 * block)
    index = block * offsets[:, None] + block - step[None, :]
    wrapped = (index + period // 2) % period - period // 2
    safe = np.where(wrapped == 0, 1, wrapped)
    sign = np.where(safe % 2 == 0, 1.0, -1.0)
    values = sign * (math.pi / period) / np.sin(math.pi * safe / period)
    values = np.where(wrapped == 0, 0.0, values)
    spectrum = np.fft.fft(values, axis=0)[: size // 2 + 1] / size
    table = np.empty((size, 2 * block))
    table[0] = spectrum[0].real
    table[1] = spectrum[size // 2].real
    table[2::2] = 2.0 * spectrum[1 : size // 2].real
    table[3::2] = 2.0 * spectrum[1 : size // 2].imag
    return table.astype(np.float32)


def split_parts(value):
    high = value.astype(BF)
    rest = value - high.astype(F32)
    mid = rest.astype(BF)
    return high, mid, (rest - mid.astype(F32)).astype(BF)


def left_lanes(shape):
    return lax.broadcasted_iota(jnp.int32, shape, len(shape) - 1) < shape[-1] // 2


def swap(value):
    return pltpu.roll(value, value.shape[-1] // 2, value.ndim - 1)


def merge(left, right):
    return jnp.where(left_lanes(left.shape), left, right)


def toeplitz_tables(spectrum, block):
    slots = spectrum.shape[0] // 2
    cuts = 4
    cut = slots // cuts

    def body(w_ref, o_ref, made, sem):
        def fill(f, _):
            for side in range(2):
                lane = w_ref[pl.ds(2 * f + side, 1), :]
                rows = jnp.broadcast_to(lane, (block, 2 * block))
                rows = pltpu.roll(rows, 0, 1, stride=1, stride_axis=0)[:, block:]
                high, mid, low = split_parts(rows)
                for p, part in enumerate((mid, high, low)):
                    made[f, p * block : (p + 1) * block, side * block : (side + 1) * block] = part
            return 0

        leave = []
        for c in range(cuts):
            lax.fori_loop(c * cut, (c + 1) * cut, fill, 0, unroll=4)
            part = pl.ds(c * cut, cut)
            leave.append(pltpu.make_async_copy(made.at[part], o_ref.at[part], sem.at[c]))
            leave[-1].start()
        for copy in leave:
            copy.wait()

    shape = (slots, 3 * block, 2 * block)
    return pl.pallas_call(
        body,
        name="toeplitz_tables",
        in_specs=[VMEM],
        out_specs=HBM,
        out_shape=jax.ShapeDtypeStruct(shape, BF),
        scratch_shapes=[pltpu.VMEM(shape, BF), pltpu.SemaphoreType.DMA((cuts,))],
        compiler_params=pltpu.CompilerParams(vmem_limit_bytes=58 << 20),
        cost_estimate=pl.CostEstimate(
            flops=slots * block * block * 32,
            bytes_accessed=slots * 3 * block * block * 4,
            transcendentals=0,
        ),
    )(spectrum)


def far_copies(count, place, stacked, pieces, sem, outward):
    rows = stacked.shape[1]
    out = []
    for k in range(count):
        other = lax.rem(place + (k if outward else count - k), count)
        mine = stacked.at[other]
        piece = pieces[k].at[pl.ds(0, rows)]
        pair = (mine, piece) if outward else (piece, mine)
        out.append(pltpu.make_async_copy(pair[0], pair[1], sem.at[k]))
    return out


def run_copies(copies):
    for copy in copies:
        copy.start()
    for copy in copies:
        copy.wait()


HBM = pl.BlockSpec(memory_space=pltpu.HBM)
SMEM = pl.BlockSpec(memory_space=pltpu.SMEM)
VMEM = pl.BlockSpec(memory_space=pltpu.VMEM)


def pack(view, chunk, count, place, carried, parts):
    per, _, half, lines = view.shape
    span = lines // 2
    width = span // count * 2
    depth = per * half
    quarter = half // 2
    steps = [(b, q * quarter) for b in range(per) for q in range(2)]

    def body(place_ref, v_ref, *refs):
        refs = list(refs)
        total = jnp.zeros((8, width), F32) if carried is None else refs.pop(0)[...]
        outs = [refs.pop(0) for _ in range(count if parts else 1)]
        sums, buf, packed, in_sem, out_sem = refs
        arrive = [
            pltpu.make_async_copy(
                v_ref.at[b, :, pl.ds(r, quarter), pl.ds(chunk * span, span)],
                buf.at[j],
                in_sem.at[j],
            )
            for j, (b, r) in enumerate(steps)
        ]
        for copy in arrive:
            copy.start()
        leave = []
        for j, (b, r) in enumerate(steps):
            arrive[j].wait()
            rows = pl.ds(b * half + r, quarter)
            for tile in range(count // 2):
                top = buf[j, 0, :, tile * width : (tile + 1) * width]
                low = buf[j, 1, :, tile * width : (tile + 1) * width]
                packed[2 * tile, rows, :] = merge(top, swap(low))
                packed[2 * tile + 1, rows, :] = merge(swap(top), low)
                square = top * top + low * low
                total += jnp.sum(square.reshape(quarter // 8, 8, width), axis=0)
            if not parts:
                leave.append(
                    pltpu.make_async_copy(packed.at[:, rows], outs[0].at[:, rows], out_sem.at[j])
                )
                leave[-1].start()
        sums[...] = total
        if parts:
            leave = far_copies(count, place_ref[0], packed, outs, out_sem, True)
            for copy in leave:
                copy.start()
        for copy in leave:
            copy.wait()

    if parts:
        outs = [jax.ShapeDtypeStruct((depth, width), F32)] * count
    else:
        outs = [jax.ShapeDtypeStruct((count, depth, width), F32)]
    result = pl.pallas_call(
        body,
        name="pack_pieces" if parts else "pack_stacked",
        in_specs=[SMEM, HBM] + [VMEM] * (carried is not None),
        out_specs=[HBM] * len(outs) + [VMEM],
        out_shape=outs + [jax.ShapeDtypeStruct((8, width), F32)],
        scratch_shapes=[
            pltpu.VMEM((len(steps), 2, quarter, span), F32),
            pltpu.VMEM((count, depth, width), F32),
            pltpu.SemaphoreType.DMA((len(steps),)),
            pltpu.SemaphoreType.DMA((max(count, len(steps)),)),
        ],
        compiler_params=pltpu.CompilerParams(vmem_limit_bytes=58 << 20),
        cost_estimate=pl.CostEstimate(
            flops=depth * lines * 2, bytes_accessed=depth * lines * 8, transcendentals=0
        ),
    )(place, view, *([] if carried is None else [carried]))
    return (list(result[:count]) if parts else result[0]), result[-1]


def line_slopes(arrived, place, gram, tables, match, sums):
    gather = isinstance(arrived, list)
    spread = sums is not None
    count = len(arrived) if gather else arrived.shape[0]
    depth, width = arrived[0].shape[-2:]
    slots, block = tables.shape[0], tables.shape[2] // 2
    half = block // 2
    per = depth // half
    out_blocks = per * count
    size = 2 * slots
    ext_rows = gram.shape[0]
    cuts = 4
    cut = slots // cuts

    def body(place_ref, g_ref, table_ref, *refs):
        refs = list(refs)
        sums_ref = refs.pop(0) if spread else None
        ins = [refs.pop(0) for _ in range(count if gather else 1)]
        outs = [refs.pop(0) for _ in range(count if spread else 1)]
        t_ref, spec, extra, lines, result, table_sem, in_sem, out_sem, sum_sem = refs
        load = [
            pltpu.make_async_copy(
                table_ref.at[pl.ds(c * cut, cut)], t_ref.at[pl.ds(c * cut, cut)], table_sem.at[c]
            )
            for c in range(cuts)
        ]
        if gather:
            copies = far_copies(count, place_ref[0], lines, ins, in_sem, False)
        else:
            copies = [pltpu.make_async_copy(ins[0], lines, in_sem.at[0])]
        for copy in copies + load:
            copy.start()
        for copy in copies:
            copy.wait()

        def at_block(b, at):
            return b // per, pl.ds((b % per) * half + at, GROUP), slice(None)

        ext = jnp.zeros((ext_rows, width), F32)
        for j in range(match):
            ext += g_ref[:, j : j + 1] * lines[0, j : j + 1, :]
        for j in range(match):
            row = depth - match + j
            tail = swap(lines[count - 1, row : row + 1, :])
            ext += g_ref[:, match + j : match + j + 1] * tail
        extra[...] = jnp.zeros_like(extra)
        extra[:ext_rows, :] = merge(ext, jnp.zeros_like(ext))

        def forward(group, _):
            at = pl.multiple_of(group * GROUP, GROUP)
            seq = [lines[at_block(b, at)] for b in range(out_blocks)]
            seq.append(extra[pl.ds(at, GROUP), :])
            out = real_transform(seq + [None] * (size - out_blocks - 1))
            spec[0, pl.ds(at, GROUP), :width] = out[0][0]
            spec[0, pl.ds(at, GROUP), width:] = out[slots][0]
            for f in range(1, slots):
                spec[f, pl.ds(at, GROUP), :width] = out[f][0]
                spec[f, pl.ds(at, GROUP), width:] = out[f][1]
            return 0

        lax.fori_loop(0, half // GROUP, forward, 0)
        for copy in load:
            copy.wait()

        def product(f, blocks):
            high, mid, low = split_parts(jnp.concatenate(blocks, 0))
            one = jnp.dot(
                t_ref[f, : 2 * block, :],
                jnp.concatenate([high, mid], 1),
                preferred_element_type=F32,
            )
            two = jnp.dot(
                t_ref[f, block:, :],
                jnp.concatenate([low, high], 1),
                preferred_element_type=F32,
            )
            small = one[:block, width:] + (two[:block, :width] + two[block:, width:])
            got = one[block:, :width] + ((one[:block, :width] + one[block:, width:]) + small)
            top, bottom = got[:half], got[half:]
            spec[f, :, :width] = merge(top, swap(bottom))
            spec[f, :, width:] = merge(swap(top), bottom)

        re, im = spec[0, :, :width], spec[0, :, width:]
        none = jnp.zeros_like(re)
        product(
            0, [merge(re, none), merge(swap(re), none), merge(none, swap(im)), merge(none, im)]
        )

        def multiply(f, _):
            re, im = spec[f, :, :width], spec[f, :, width:]
            re_s, im_s = swap(re), swap(im)
            product(f, [merge(re, im_s), merge(re_s, im), merge(-im, re_s), merge(-im_s, re)])
            return 0

        lax.fori_loop(1, slots, multiply, 0, unroll=8)

        def backward(group, _):
            at = pl.multiple_of(group * GROUP, GROUP)
            values = [(spec[0, pl.ds(at, GROUP), :width], None)]
            for f in range(1, slots):
                values.append(
                    (spec[f, pl.ds(at, GROUP), :width], spec[f, pl.ds(at, GROUP), width:])
                )
            values.append((spec[0, pl.ds(at, GROUP), width:], None))
            for b, value in enumerate(real_inverse(values, size, out_blocks)):
                result[at_block(b, at)] = value
            return 0

        lax.fori_loop(0, half // GROUP, backward, 0)
        if spread:
            copies = far_copies(count, place_ref[0], result, outs, out_sem, True)
            for k in range(count):
                below = outs[k].at[pl.ds(depth, 8)]
                copies.append(pltpu.make_async_copy(sums_ref, below, sum_sem.at[k]))
        else:
            copies = [pltpu.make_async_copy(result, outs[0], out_sem.at[0])]
        run_copies(copies)

    if spread:
        out_shape = [jax.ShapeDtypeStruct((depth + 8, width), F32)] * count
    else:
        out_shape = [jax.ShapeDtypeStruct((count, depth, width), F32)]
    stacked = pltpu.VMEM((count, depth, width), F32)
    out = pl.pallas_call(
        body,
        name="line_slopes",
        in_specs=[SMEM, VMEM, HBM] + [VMEM] * spread + [HBM] * (count if gather else 1),
        out_specs=[HBM] * len(out_shape),
        out_shape=out_shape,
        scratch_shapes=[
            pltpu.VMEM(tables.shape, BF),
            pltpu.VMEM((slots, half, 2 * width), F32),
            pltpu.VMEM((half, width), F32),
            stacked,
            stacked,
            pltpu.SemaphoreType.DMA((cuts,)),
            pltpu.SemaphoreType.DMA((count,)),
            pltpu.SemaphoreType.DMA((count,)),
            pltpu.SemaphoreType.DMA((count,)),
        ],
        compiler_params=pltpu.CompilerParams(vmem_limit_bytes=50 << 20),
        cost_estimate=pl.CostEstimate(
            flops=16 * size * block * block * width,
            bytes_accessed=8 * count * depth * width,
            transcendentals=0,
        ),
    )(place, gram, tables, *([sums] if spread else []), *(arrived if gather else [arrived]))
    return list(out) if spread else out[0]


def advect(view, chunk, arrived, place, points, energy, earlier):
    gather = isinstance(arrived, list)
    per, _, half, lines = view.shape
    span = lines // 2
    count = len(arrived) if gather else arrived.shape[0]
    depth, width = per * half, arrived[0].shape[-1]
    quarter = half // 2
    steps = [(b, q * quarter) for b in range(per) for q in range(2)]
    kept = 0 if earlier is None else 2

    def body(place_ref, v_ref, *refs):
        refs = list(refs)[kept:]
        energy_in = None if gather else refs.pop(0)
        ins = [refs.pop(0) for _ in range(count if gather else 1)]
        s_ref, f_ref = refs.pop(0), refs.pop(0)
        energy_out = refs.pop(0) if gather else None
        v_buf, stacked, tiles, s_buf, f_buf, v_sem, in_sem, sum_sem, s_sem, f_sem = refs

        def part(ref, j):
            b, r = steps[j]
            return ref.at[b, :, pl.ds(r, quarter), pl.ds(chunk * span, span)]

        fields = [
            pltpu.make_async_copy(part(v_ref, j), v_buf.at[j], v_sem.at[j])
            for j in range(len(steps))
        ]
        if gather:
            pieces = far_copies(count, place_ref[0], stacked, ins, in_sem, False)
            for k in range(count):
                below = ins[k].at[pl.ds(depth, 8)]
                pieces.append(pltpu.make_async_copy(below, tiles.at[k], sum_sem.at[k]))
        else:
            pieces = [pltpu.make_async_copy(ins[0], stacked, in_sem.at[0])]
        for copy in pieces + fields:
            copy.start()
        for copy in pieces:
            copy.wait()
        if gather:
            tile = tiles[0]
            for k in range(1, count):
                tile += tiles[k]
            energy_out[...] = tile
        else:
            tile = energy_in[...]
        lane_sum = jnp.sum(tile, axis=0, keepdims=True)
        mean_square = jnp.sum(lane_sum, axis=1, keepdims=True) / points
        rate = jnp.broadcast_to(courant / jnp.sqrt(mean_square + epsilon), (quarter, width))
        leave = []
        for j, (b, r) in enumerate(steps):
            fields[j].wait()
            rows = pl.ds(b * half + r, quarter)
            for tile in range(count // 2):
                lanes = slice(tile * width, (tile + 1) * width)
                one = stacked[2 * tile, rows, :]
                two = stacked[2 * tile + 1, rows, :]
                for side, slope in enumerate((merge(one, swap(two)), merge(swap(one), two))):
                    field = v_buf[j, side, :, lanes]
                    s_buf[j, side, :, lanes] = slope
                    f_buf[j, side, :, lanes] = field - rate * field * slope
            leave.append(pltpu.make_async_copy(s_buf.at[j], part(s_ref, j), s_sem.at[j]))
            leave.append(pltpu.make_async_copy(f_buf.at[j], part(f_ref, j), f_sem.at[j]))
            leave[-2].start()
            leave[-1].start()
        for copy in leave:
            copy.wait()

    buffer = pltpu.VMEM((len(steps), 2, quarter, span), F32)
    step_sem = pltpu.SemaphoreType.DMA((len(steps),))
    piece_sem = pltpu.SemaphoreType.DMA((count,))
    out = pl.pallas_call(
        body,
        name="advect",
        in_specs=[SMEM, HBM]
        + [HBM] * kept
        + ([HBM] * count if gather else [VMEM, HBM]),
        out_specs=[HBM, HBM] + [VMEM] * gather,
        out_shape=[jax.ShapeDtypeStruct(view.shape, F32)] * 2
        + [jax.ShapeDtypeStruct((8, width), F32)] * gather,
        scratch_shapes=[
            buffer,
            pltpu.VMEM((count, depth, width), F32),
            pltpu.VMEM((count, 8, width), F32),
            buffer,
            buffer,
            step_sem,
            piece_sem,
            piece_sem,
            step_sem,
            step_sem,
        ],
        input_output_aliases={2: 0, 3: 1} if kept else {},
        compiler_params=pltpu.CompilerParams(vmem_limit_bytes=12 << 20),
        cost_estimate=pl.CostEstimate(
            flops=depth * lines * 3, bytes_accessed=depth * lines * 16, transcendentals=0
        ),
    )(place, view, *(earlier or ()), *(arrived if gather else [energy, arrived]))
    return out[:2], (out[2] if gather else energy)


def exchange(pieces, axis):
    if not isinstance(pieces, list):
        return lax.all_to_all(pieces, axis, split_axis=0, concat_axis=0, tiled=True)
    count = len(pieces)
    out = [pieces[0]]
    for k in range(1, count):
        moved = lax.ppermute(pieces[k], axis, [(i, (i + k) % count) for i in range(count)])
        out.append(moved)
    return out


def total_over(part, axis):
    size = lax.axis_size(axis)
    moving = part
    for _ in range(size - 1):
        moving = lax.ppermute(moving, axis, [(i, (i + 1) % size) for i in range(size)])
        part = part + moving
    return part


def per_device(velocity, left_gram, right_gram):
    row_count, line_total = velocity.shape
    cont, match = left_gram.shape
    gx_count = lax.axis_size("gx")
    ga_count = lax.axis_size("ga")
    place = lax.axis_index("gx").astype(jnp.int32).reshape(1)
    total = row_count * gx_count
    block = 2 * LANE
    while row_count % block or block > LANE:
        block //= 2
    half = block // 2
    assert cont <= half and match <= half and line_total % (gx_count * LANE) == 0
    out_blocks = total // block
    size = transform_size(2 * out_blocks)
    view = velocity.reshape(row_count // block, 2, half, line_total)

    points = row_count * line_total * gx_count * ga_count

    first, sums = pack(view, 0, gx_count, place, None, True)
    first = exchange(first, "gx")
    second, sums = pack(view, 1, gx_count, place, sums, False)
    sums = total_over(sums, "ga")
    spectrum = slope_spectrum(total + cont, block, out_blocks, size)
    tables = toeplitz_tables(jnp.asarray(spectrum), block)
    second, tables = lax.optimization_barrier((second, tables))
    second = exchange(second, "gx")
    gram = jnp.concatenate([left_gram, right_gram], axis=1)
    gram = jnp.pad(gram, ((0, -cont % 8), (0, 0)))
    first = line_slopes(first, place, gram, tables, match, sums)
    first = exchange(first, "gx")
    second = line_slopes(second, place, gram, tables, match, None)
    second = exchange(second, "gx")
    done, energy = advect(view, 0, first, place, points, None, None)
    done, _ = advect(view, 1, second, place, points, energy, done)
    return tuple(part.reshape(row_count, line_total) for part in done)


def solution(mesh):
    return jax.shard_map(
        per_device,
        mesh=mesh,
        in_specs=(P("gx", "ga"), P(), P()),
        out_specs=(P("gx", "ga"), P("gx", "ga")),
        check_vma=False,
    )
```

```python
import math

import jax
import jax.numpy as jnp
import numpy as np
from jax import lax
from jax.experimental import pallas as pl
from jax.experimental.pallas import tpu as pltpu
from jax.sharding import PartitionSpec as P

courant = 0.5
epsilon = 1e-06
LANE = 128
GROUP = 8
BF = jnp.bfloat16
F32 = jnp.float32


def add(a, b):
    return b if a is None else a if b is None else a + b


def sub(a, b):
    return a if b is None else -b if a is None else a - b


def scale(a, c):
    return None if a is None else a * np.float32(c)


def turn(value, angle):
    c, s = math.cos(angle), math.sin(angle)
    re, im = value
    return (sub(scale(re, c), scale(im, s)), add(scale(im, c), scale(re, s)))


def real_transform(seq):
    size = len(seq)
    if size == 1:
        return [(seq[0], None)]
    if size == 3:
        far = add(seq[1], seq[2])
        gap = sub(seq[1], seq[2])
        return [
            (add(seq[0], far), None),
            (sub(seq[0], scale(far, 0.5)), scale(gap, -math.sqrt(0.75))),
        ]
    even = real_transform(seq[0::2])
    odd = real_transform(seq[1::2])
    out = [None] * (size // 2 + 1)
    for f in range((size + 3) // 4):
        e = even[f]
        o = odd[f] if f == 0 else turn(odd[f], -2.0 * math.pi * f / size)
        out[f] = (add(e[0], o[0]), add(e[1], o[1]))
        out[size // 2 - f] = (sub(e[0], o[0]), sub(o[1], e[1]))
    if size % 4 == 0:
        f = size // 4
        out[f] = (even[f][0], scale(odd[f][0], -1.0))
    return out


def real_inverse(spec, size, count):
    if count <= 0:
        return []
    if size == 1:
        return [spec[0][0]]
    if size == 3:
        out = [add(spec[0][0], spec[1][0])]
        if count > 1:
            base = sub(spec[0][0], scale(spec[1][0], 0.5))
            side = scale(spec[1][1], math.sqrt(0.75))
            out.append(sub(base, side))
            out.append(add(base, side))
        return out[:count]
    half = size // 2
    even = [None] * (half // 2 + 1)
    odd = [None] * (half // 2 + 1)
    for f in range((size + 3) // 4):
        a, b = spec[f], spec[half - f]
        even[f] = (add(a[0], b[0]), sub(a[1], b[1]))
        diff = (sub(a[0], b[0]), add(a[1], b[1]))
        odd[f] = diff if f == 0 else turn(diff, 2.0 * math.pi * f / size)
    if size % 4 == 0:
        f = size // 4
        even[f] = (spec[f][0], None)
        odd[f] = (scale(spec[f][1], -1.0), None)
    first = real_inverse(even, half, (count + 1) // 2)
    second = real_inverse(odd, half, count // 2)
    out = [None] * count
    out[0::2] = first
    out[1::2] = second
    return out


def transform_size(least):
    size = 1
    while True:
        if size >= least:
            return size
        if size % 2 == 0 and size // 2 * 3 >= least:
            return size // 2 * 3
        size *= 2


def slope_spectrum(period, block, out_blocks, size):
    offsets = np.arange(size)
    offsets = np.where(offsets < out_blocks, offsets, offsets - size)
    step = np.arange(2 * block)
    index = block * offsets[:, None] + block - step[None, :]
    wrapped = (index + period // 2) % period - period // 2
    safe = np.where(wrapped == 0, 1, wrapped)
    sign = np.where(safe % 2 == 0, 1.0, -1.0)
    values = sign * (math.pi / period) / np.sin(math.pi * safe / period)
    values = np.where(wrapped == 0, 0.0, values)
    spectrum = np.fft.fft(values, axis=0)[: size // 2 + 1] / size
    table = np.empty((size, 2 * block))
    table[0] = spectrum[0].real
    table[1] = spectrum[size // 2].real
    table[2::2] = 2.0 * spectrum[1 : size // 2].real
    table[3::2] = 2.0 * spectrum[1 : size // 2].imag
    return table.astype(np.float32)


def split_parts(value):
    high = value.astype(BF)
    rest = value - high.astype(F32)
    mid = rest.astype(BF)
    return high, mid, (rest - mid.astype(F32)).astype(BF)


def left_lanes(shape):
    return lax.broadcasted_iota(jnp.int32, shape, len(shape) - 1) < shape[-1] // 2


def swap(value):
    return pltpu.roll(value, value.shape[-1] // 2, value.ndim - 1)


def merge(left, right):
    return jnp.where(left_lanes(left.shape), left, right)


def toeplitz_tables(spectrum, block):
    slots = spectrum.shape[0] // 2
    cuts = 4
    cut = slots // cuts

    def body(w_ref, o_ref, made, sem):
        def fill(f, _):
            for side in range(2):
                lane = w_ref[pl.ds(2 * f + side, 1), :]
                rows = jnp.broadcast_to(lane, (block, 2 * block))
                rows = pltpu.roll(rows, 0, 1, stride=1, stride_axis=0)[:, block:]
                high, mid, low = split_parts(rows)
                for p, part in enumerate((mid, high, low)):
                    made[f, p * block : (p + 1) * block, side * block : (side + 1) * block] = part
            return 0

        leave = []
        for c in range(cuts):
            lax.fori_loop(c * cut, (c + 1) * cut, fill, 0, unroll=4)
            part = pl.ds(c * cut, cut)
            leave.append(pltpu.make_async_copy(made.at[part], o_ref.at[part], sem.at[c]))
            leave[-1].start()
        for copy in leave:
            copy.wait()

    shape = (slots, 3 * block, 2 * block)
    return pl.pallas_call(
        body,
        name="toeplitz_tables",
        in_specs=[VMEM],
        out_specs=HBM,
        out_shape=jax.ShapeDtypeStruct(shape, BF),
        scratch_shapes=[pltpu.VMEM(shape, BF), pltpu.SemaphoreType.DMA((cuts,))],
        compiler_params=pltpu.CompilerParams(vmem_limit_bytes=58 << 20),
        cost_estimate=pl.CostEstimate(
            flops=slots * block * block * 32,
            bytes_accessed=slots * 3 * block * block * 4,
            transcendentals=0,
        ),
    )(spectrum)


def far_copies(count, place, stacked, pieces, sem, outward):
    rows = stacked.shape[1]
    out = []
    for k in range(count):
        other = lax.rem(place + (k if outward else count - k), count)
        mine = stacked.at[other]
        piece = pieces[k].at[pl.ds(0, rows)]
        pair = (mine, piece) if outward else (piece, mine)
        out.append(pltpu.make_async_copy(pair[0], pair[1], sem.at[k]))
    return out


def run_copies(copies):
    for copy in copies:
        copy.start()
    for copy in copies:
        copy.wait()


HBM = pl.BlockSpec(memory_space=pltpu.HBM)
SMEM = pl.BlockSpec(memory_space=pltpu.SMEM)
VMEM = pl.BlockSpec(memory_space=pltpu.VMEM)


def pack(view, chunk, count, place, carried, parts):
    per, _, half, lines = view.shape
    span = lines // 2
    width = span // count * 2
    depth = per * half
    quarter = half // 2
    steps = [(b, q * quarter) for b in range(per) for q in range(2)]

    def body(place_ref, v_ref, *refs):
        refs = list(refs)
        total = jnp.zeros((8, width), F32) if carried is None else refs.pop(0)[...]
        outs = [refs.pop(0) for _ in range(count if parts else 1)]
        sums, buf, packed, in_sem, out_sem = refs
        arrive = [
            pltpu.make_async_copy(
                v_ref.at[b, :, pl.ds(r, quarter), pl.ds(chunk * span, span)],
                buf.at[j],
                in_sem.at[j],
            )
            for j, (b, r) in enumerate(steps)
        ]
        for copy in arrive:
            copy.start()
        leave = []
        for j, (b, r) in enumerate(steps):
            arrive[j].wait()
            rows = pl.ds(b * half + r, quarter)
            for tile in range(count // 2):
                top = buf[j, 0, :, tile * width : (tile + 1) * width]
                low = buf[j, 1, :, tile * width : (tile + 1) * width]
                packed[2 * tile, rows, :] = merge(top, swap(low))
                packed[2 * tile + 1, rows, :] = merge(swap(top), low)
                square = top * top + low * low
                total += jnp.sum(square.reshape(quarter // 8, 8, width), axis=0)
            if not parts:
                leave.append(
                    pltpu.make_async_copy(packed.at[:, rows], outs[0].at[:, rows], out_sem.at[j])
                )
                leave[-1].start()
        sums[...] = total
        if parts:
            leave = far_copies(count, place_ref[0], packed, outs, out_sem, True)
            for copy in leave:
                copy.start()
        for copy in leave:
            copy.wait()

    if parts:
        outs = [jax.ShapeDtypeStruct((depth, width), F32)] * count
    else:
        outs = [jax.ShapeDtypeStruct((count, depth, width), F32)]
    result = pl.pallas_call(
        body,
        name="pack_pieces" if parts else "pack_stacked",
        in_specs=[SMEM, HBM] + [VMEM] * (carried is not None),
        out_specs=[HBM] * len(outs) + [VMEM],
        out_shape=outs + [jax.ShapeDtypeStruct((8, width), F32)],
        scratch_shapes=[
            pltpu.VMEM((len(steps), 2, quarter, span), F32),
            pltpu.VMEM((count, depth, width), F32),
            pltpu.SemaphoreType.DMA((len(steps),)),
            pltpu.SemaphoreType.DMA((max(count, len(steps)),)),
        ],
        compiler_params=pltpu.CompilerParams(vmem_limit_bytes=58 << 20),
        cost_estimate=pl.CostEstimate(
            flops=depth * lines * 2, bytes_accessed=depth * lines * 8, transcendentals=0
        ),
    )(place, view, *([] if carried is None else [carried]))
    return (list(result[:count]) if parts else result[0]), result[-1]


def line_slopes(arrived, place, gram, tables, match, sums):
    gather = isinstance(arrived, list)
    below = 0 if sums is None else 8
    count = len(arrived) if gather else arrived.shape[0]
    depth, width = arrived[0].shape[-2:]
    slots, block = tables.shape[0], tables.shape[2] // 2
    half = block // 2
    per = depth // half
    out_blocks = per * count
    size = 2 * slots
    ext_rows = gram.shape[0]
    cuts = 4
    cut = slots // cuts

    def body(place_ref, g_ref, table_ref, *refs):
        refs = list(refs)
        sums_ref = refs.pop(0) if below else None
        ins = [refs.pop(0) for _ in range(count if gather else 1)]
        outs = [refs.pop(0) for _ in range(count)]
        t_ref, spec, extra, lines, result, table_sem, in_sem, out_sem, sum_sem = refs
        load = [
            pltpu.make_async_copy(
                table_ref.at[pl.ds(c * cut, cut)], t_ref.at[pl.ds(c * cut, cut)], table_sem.at[c]
            )
            for c in range(cuts)
        ]
        if gather:
            copies = far_copies(count, place_ref[0], lines, ins, in_sem, False)
        else:
            copies = [pltpu.make_async_copy(ins[0], lines, in_sem.at[0])]
        for copy in copies + load:
            copy.start()
        for copy in copies:
            copy.wait()

        def at_block(b, at):
            return b // per, pl.ds((b % per) * half + at, GROUP), slice(None)

        ext = jnp.zeros((ext_rows, width), F32)
        for j in range(match):
            ext += g_ref[:, j : j + 1] * lines[0, j : j + 1, :]
        for j in range(match):
            row = depth - match + j
            tail = swap(lines[count - 1, row : row + 1, :])
            ext += g_ref[:, match + j : match + j + 1] * tail
        extra[...] = jnp.zeros_like(extra)
        extra[:ext_rows, :] = merge(ext, jnp.zeros_like(ext))

        def forward(group, _):
            at = pl.multiple_of(group * GROUP, GROUP)
            seq = [lines[at_block(b, at)] for b in range(out_blocks)]
            seq.append(extra[pl.ds(at, GROUP), :])
            out = real_transform(seq + [None] * (size - out_blocks - 1))
            spec[0, pl.ds(at, GROUP), :width] = out[0][0]
            spec[0, pl.ds(at, GROUP), width:] = out[slots][0]
            for f in range(1, slots):
                spec[f, pl.ds(at, GROUP), :width] = out[f][0]
                spec[f, pl.ds(at, GROUP), width:] = out[f][1]
            return 0

        lax.fori_loop(0, half // GROUP, forward, 0)
        for copy in load:
            copy.wait()

        def product(f, blocks):
            high, mid, low = split_parts(jnp.concatenate(blocks, 0))
            one = jnp.dot(
                t_ref[f, : 2 * block, :],
                jnp.concatenate([high, mid], 1),
                preferred_element_type=F32,
            )
            two = jnp.dot(
                t_ref[f, block:, :],
                jnp.concatenate([low, high], 1),
                preferred_element_type=F32,
            )
            small = one[:block, width:] + (two[:block, :width] + two[block:, width:])
            got = one[block:, :width] + ((one[:block, :width] + one[block:, width:]) + small)
            top, bottom = got[:half], got[half:]
            spec[f, :, :width] = merge(top, swap(bottom))
            spec[f, :, width:] = merge(swap(top), bottom)

        re, im = spec[0, :, :width], spec[0, :, width:]
        none = jnp.zeros_like(re)
        product(
            0, [merge(re, none), merge(swap(re), none), merge(none, swap(im)), merge(none, im)]
        )

        def multiply(f, _):
            re, im = spec[f, :, :width], spec[f, :, width:]
            re_s, im_s = swap(re), swap(im)
            product(f, [merge(re, im_s), merge(re_s, im), merge(-im, re_s), merge(-im_s, re)])
            return 0

        lax.fori_loop(1, slots, multiply, 0, unroll=8)

        def backward(group, _):
            at = pl.multiple_of(group * GROUP, GROUP)
            values = [(spec[0, pl.ds(at, GROUP), :width], None)]
            for f in range(1, slots):
                values.append(
                    (spec[f, pl.ds(at, GROUP), :width], spec[f, pl.ds(at, GROUP), width:])
                )
            values.append((spec[0, pl.ds(at, GROUP), width:], None))
            for b, value in enumerate(real_inverse(values, size, out_blocks)):
                result[at_block(b, at)] = value
            return 0

        lax.fori_loop(0, half // GROUP, backward, 0)
        copies = far_copies(count, place_ref[0], result, outs, out_sem, True)
        if below:
            for k in range(count):
                under = outs[k].at[pl.ds(depth, below)]
                copies.append(pltpu.make_async_copy(sums_ref, under, sum_sem.at[k]))
        run_copies(copies)

    out_shape = [jax.ShapeDtypeStruct((depth + below, width), F32)] * count
    stacked = pltpu.VMEM((count, depth, width), F32)
    out = pl.pallas_call(
        body,
        name="line_slopes",
        in_specs=[SMEM, VMEM, HBM] + [VMEM] * (sums is not None) + [HBM] * (count if gather else 1),
        out_specs=[HBM] * len(out_shape),
        out_shape=out_shape,
        scratch_shapes=[
            pltpu.VMEM(tables.shape, BF),
            pltpu.VMEM((slots, half, 2 * width), F32),
            pltpu.VMEM((half, width), F32),
            stacked,
            stacked,
            pltpu.SemaphoreType.DMA((cuts,)),
            pltpu.SemaphoreType.DMA((count,)),
            pltpu.SemaphoreType.DMA((count,)),
            pltpu.SemaphoreType.DMA((count,)),
        ],
        compiler_params=pltpu.CompilerParams(vmem_limit_bytes=50 << 20),
        cost_estimate=pl.CostEstimate(
            flops=16 * size * block * block * width,
            bytes_accessed=8 * count * depth * width,
            transcendentals=0,
        ),
    )(place, gram, tables, *([sums] if below else []), *(arrived if gather else [arrived]))
    return list(out)


def advect(view, chunk, arrived, place, points, energy, earlier):
    adding = energy is None
    per, _, half, lines = view.shape
    span = lines // 2
    count = len(arrived)
    depth, width = per * half, arrived[0].shape[-1]
    quarter = half // 2
    steps = [(b, q * quarter) for b in range(per) for q in range(2)]
    kept = 0 if earlier is None else 2

    def body(place_ref, v_ref, *refs):
        refs = list(refs)[kept:]
        energy_in = None if adding else refs.pop(0)
        ins = [refs.pop(0) for _ in range(count)]
        s_ref, f_ref = refs.pop(0), refs.pop(0)
        energy_out = refs.pop(0) if adding else None
        v_buf, stacked, tiles, s_buf, f_buf, v_sem, in_sem, sum_sem, s_sem, f_sem = refs

        def part(ref, j):
            b, r = steps[j]
            return ref.at[b, :, pl.ds(r, quarter), pl.ds(chunk * span, span)]

        fields = [
            pltpu.make_async_copy(part(v_ref, j), v_buf.at[j], v_sem.at[j])
            for j in range(len(steps))
        ]
        pieces = far_copies(count, place_ref[0], stacked, ins, in_sem, False)
        if adding:
            for k in range(count):
                below = ins[k].at[pl.ds(depth, 8)]
                pieces.append(pltpu.make_async_copy(below, tiles.at[k], sum_sem.at[k]))
        for copy in pieces + fields:
            copy.start()
        for copy in pieces:
            copy.wait()
        if adding:
            tile = tiles[0]
            for k in range(1, count):
                tile += tiles[k]
            energy_out[...] = tile
        else:
            tile = energy_in[...]
        lane_sum = jnp.sum(tile, axis=0, keepdims=True)
        mean_square = jnp.sum(lane_sum, axis=1, keepdims=True) / points
        rate = jnp.broadcast_to(courant / jnp.sqrt(mean_square + epsilon), (quarter, width))
        leave = []
        for j, (b, r) in enumerate(steps):
            fields[j].wait()
            rows = pl.ds(b * half + r, quarter)
            for tile in range(count // 2):
                lanes = slice(tile * width, (tile + 1) * width)
                one = stacked[2 * tile, rows, :]
                two = stacked[2 * tile + 1, rows, :]
                for side, slope in enumerate((merge(one, swap(two)), merge(swap(one), two))):
                    field = v_buf[j, side, :, lanes]
                    s_buf[j, side, :, lanes] = slope
                    f_buf[j, side, :, lanes] = field - rate * field * slope
            leave.append(pltpu.make_async_copy(s_buf.at[j], part(s_ref, j), s_sem.at[j]))
            leave.append(pltpu.make_async_copy(f_buf.at[j], part(f_ref, j), f_sem.at[j]))
            leave[-2].start()
            leave[-1].start()
        for copy in leave:
            copy.wait()

    buffer = pltpu.VMEM((len(steps), 2, quarter, span), F32)
    step_sem = pltpu.SemaphoreType.DMA((len(steps),))
    piece_sem = pltpu.SemaphoreType.DMA((count,))
    out = pl.pallas_call(
        body,
        name="advect",
        in_specs=[SMEM, HBM]
        + [HBM] * kept
        + [VMEM] * (not adding)
        + [HBM] * count,
        out_specs=[HBM, HBM] + [VMEM] * adding,
        out_shape=[jax.ShapeDtypeStruct(view.shape, F32)] * 2
        + [jax.ShapeDtypeStruct((8, width), F32)] * adding,
        scratch_shapes=[
            buffer,
            pltpu.VMEM((count, depth, width), F32),
            pltpu.VMEM((count, 8, width), F32),
            buffer,
            buffer,
            step_sem,
            piece_sem,
            piece_sem,
            step_sem,
            step_sem,
        ],
        input_output_aliases={2: 0, 3: 1} if kept else {},
        compiler_params=pltpu.CompilerParams(vmem_limit_bytes=12 << 20),
        cost_estimate=pl.CostEstimate(
            flops=depth * lines * 3, bytes_accessed=depth * lines * 16, transcendentals=0
        ),
    )(place, view, *(earlier or ()), *(() if adding else [energy]), *arrived)
    return out[:2], (out[2] if adding else energy)


def exchange(pieces, axis):
    if not isinstance(pieces, list):
        return lax.all_to_all(pieces, axis, split_axis=0, concat_axis=0, tiled=True)
    count = len(pieces)
    out = [pieces[0]]
    for k in range(1, count):
        moved = lax.ppermute(pieces[k], axis, [(i, (i + k) % count) for i in range(count)])
        out.append(moved)
    return out


def total_over(part, axis):
    size = lax.axis_size(axis)
    moving = part
    for _ in range(size - 1):
        moving = lax.ppermute(moving, axis, [(i, (i + 1) % size) for i in range(size)])
        part = part + moving
    return part


def per_device(velocity, left_gram, right_gram):
    row_count, line_total = velocity.shape
    cont, match = left_gram.shape
    gx_count = lax.axis_size("gx")
    ga_count = lax.axis_size("ga")
    place = lax.axis_index("gx").astype(jnp.int32).reshape(1)
    total = row_count * gx_count
    block = 2 * LANE
    while row_count % block or block > LANE:
        block //= 2
    half = block // 2
    assert cont <= half and match <= half and line_total % (gx_count * LANE) == 0
    out_blocks = total // block
    size = transform_size(2 * out_blocks)
    view = velocity.reshape(row_count // block, 2, half, line_total)

    points = row_count * line_total * gx_count * ga_count

    first, sums = pack(view, 0, gx_count, place, None, True)
    first = exchange(first, "gx")
    second, sums = pack(view, 1, gx_count, place, sums, False)
    sums = total_over(sums, "ga")
    spectrum = slope_spectrum(total + cont, block, out_blocks, size)
    tables = toeplitz_tables(jnp.asarray(spectrum), block)
    second, tables = lax.optimization_barrier((second, tables))
    second = exchange(second, "gx")
    gram = jnp.concatenate([left_gram, right_gram], axis=1)
    gram = jnp.pad(gram, ((0, -cont % 8), (0, 0)))
    first = line_slopes(first, place, gram, tables, match, sums)
    first = exchange(first, "gx")
    second = line_slopes(second, place, gram, tables, match, None)
    second = exchange(second, "gx")
    done, energy = advect(view, 0, first, place, points, None, None)
    done, _ = advect(view, 1, second, place, points, energy, done)
    return tuple(part.reshape(row_count, line_total) for part in done)


def solution(mesh):
    return jax.shard_map(
        per_device,
        mesh=mesh,
        in_specs=(P("gx", "ga"), P(), P()),
        out_specs=(P("gx", "ga"), P("gx", "ga")),
        check_vma=False,
    )
```

```python
import math

import jax
import jax.numpy as jnp
import numpy as np
from jax import lax
from jax.experimental import pallas as pl
from jax.experimental.pallas import tpu as pltpu
from jax.sharding import PartitionSpec as P

courant = 0.5
epsilon = 1e-06
LANE = 128
GROUP = 8
BF = jnp.bfloat16
F32 = jnp.float32


def add(a, b):
    return b if a is None else a if b is None else a + b


def sub(a, b):
    return a if b is None else -b if a is None else a - b


def scale(a, c):
    return None if a is None else a * np.float32(c)


def turn(value, angle):
    c, s = math.cos(angle), math.sin(angle)
    re, im = value
    return (sub(scale(re, c), scale(im, s)), add(scale(im, c), scale(re, s)))


def real_transform(seq):
    size = len(seq)
    if size == 1:
        return [(seq[0], None)]
    if size == 3:
        far = add(seq[1], seq[2])
        gap = sub(seq[1], seq[2])
        return [
            (add(seq[0], far), None),
            (sub(seq[0], scale(far, 0.5)), scale(gap, -math.sqrt(0.75))),
        ]
    even = real_transform(seq[0::2])
    odd = real_transform(seq[1::2])
    out = [None] * (size // 2 + 1)
    for f in range((size + 3) // 4):
        e = even[f]
        o = odd[f] if f == 0 else turn(odd[f], -2.0 * math.pi * f / size)
        out[f] = (add(e[0], o[0]), add(e[1], o[1]))
        out[size // 2 - f] = (sub(e[0], o[0]), sub(o[1], e[1]))
    if size % 4 == 0:
        f = size // 4
        out[f] = (even[f][0], scale(odd[f][0], -1.0))
    return out


def real_inverse(spec, size, count):
    if count <= 0:
        return []
    if size == 1:
        return [spec[0][0]]
    if size == 3:
        out = [add(spec[0][0], spec[1][0])]
        if count > 1:
            base = sub(spec[0][0], scale(spec[1][0], 0.5))
            side = scale(spec[1][1], math.sqrt(0.75))
            out.append(sub(base, side))
            out.append(add(base, side))
        return out[:count]
    half = size // 2
    even = [None] * (half // 2 + 1)
    odd = [None] * (half // 2 + 1)
    for f in range((size + 3) // 4):
        a, b = spec[f], spec[half - f]
        even[f] = (add(a[0], b[0]), sub(a[1], b[1]))
        diff = (sub(a[0], b[0]), add(a[1], b[1]))
        odd[f] = diff if f == 0 else turn(diff, 2.0 * math.pi * f / size)
    if size % 4 == 0:
        f = size // 4
        even[f] = (spec[f][0], None)
        odd[f] = (scale(spec[f][1], -1.0), None)
    first = real_inverse(even, half, (count + 1) // 2)
    second = real_inverse(odd, half, count // 2)
    out = [None] * count
    out[0::2] = first
    out[1::2] = second
    return out


def transform_size(least):
    size = 1
    while True:
        if size >= least:
            return size
        if size % 2 == 0 and size // 2 * 3 >= least:
            return size // 2 * 3
        size *= 2


def slope_spectrum(period, block, out_blocks, size):
    offsets = np.arange(size)
    offsets = np.where(offsets < out_blocks, offsets, offsets - size)
    step = np.arange(2 * block)
    index = block * offsets[:, None] + block - step[None, :]
    wrapped = (index + period // 2) % period - period // 2
    safe = np.where(wrapped == 0, 1, wrapped)
    sign = np.where(safe % 2 == 0, 1.0, -1.0)
    values = sign * (math.pi / period) / np.sin(math.pi * safe / period)
    values = np.where(wrapped == 0, 0.0, values)
    spectrum = np.fft.fft(values, axis=0)[: size // 2 + 1] / size
    table = np.empty((size, 2 * block))
    table[0] = spectrum[0].real
    table[1] = spectrum[size // 2].real
    table[2::2] = 2.0 * spectrum[1 : size // 2].real
    table[3::2] = 2.0 * spectrum[1 : size // 2].imag
    return table.astype(np.float32)


def split_parts(value):
    high = value.astype(BF)
    rest = value - high.astype(F32)
    mid = rest.astype(BF)
    return high, mid, (rest - mid.astype(F32)).astype(BF)


def left_lanes(shape):
    return lax.broadcasted_iota(jnp.int32, shape, len(shape) - 1) < shape[-1] // 2


def swap(value):
    return pltpu.roll(value, value.shape[-1] // 2, value.ndim - 1)


def merge(left, right):
    return jnp.where(left_lanes(left.shape), left, right)


def toeplitz_tables(spectrum, block):
    slots = spectrum.shape[0] // 2
    cuts = 4
    cut = slots // cuts

    def body(w_ref, o_ref, made, sem):
        def fill(f, _):
            for side in range(2):
                lane = w_ref[pl.ds(2 * f + side, 1), :]
                rows = jnp.broadcast_to(lane, (block, 2 * block))
                rows = pltpu.roll(rows, 0, 1, stride=1, stride_axis=0)[:, block:]
                high, mid, low = split_parts(rows)
                for p, part in enumerate((mid, high, low)):
                    made[f, p * block : (p + 1) * block, side * block : (side + 1) * block] = part
            return 0

        leave = []
        for c in range(cuts):
            lax.fori_loop(c * cut, (c + 1) * cut, fill, 0, unroll=4)
            part = pl.ds(c * cut, cut)
            leave.append(pltpu.make_async_copy(made.at[part], o_ref.at[part], sem.at[c]))
            leave[-1].start()
        for copy in leave:
            copy.wait()

    shape = (slots, 3 * block, 2 * block)
    return pl.pallas_call(
        body,
        name="toeplitz_tables",
        in_specs=[VMEM],
        out_specs=HBM,
        out_shape=jax.ShapeDtypeStruct(shape, BF),
        scratch_shapes=[pltpu.VMEM(shape, BF), pltpu.SemaphoreType.DMA((cuts,))],
        compiler_params=pltpu.CompilerParams(vmem_limit_bytes=58 << 20),
        cost_estimate=pl.CostEstimate(
            flops=slots * block * block * 32,
            bytes_accessed=slots * 3 * block * block * 4,
            transcendentals=0,
        ),
    )(spectrum)


def far_copies(count, place, stacked, pieces, sem, outward, batch):
    size = stacked.shape[1] // 2
    rows = pl.ds(batch * size, size)
    out = []
    for k in range(count):
        other = lax.rem(place + (k if outward else count - k), count)
        mine = stacked.at[other, rows]
        piece = pieces[k].at[rows]
        pair = (mine, piece) if outward else (piece, mine)
        out.append(pltpu.make_async_copy(pair[0], pair[1], sem.at[batch * count + k]))
    return out


def start_all(copies):
    for copy in copies:
        copy.start()


def wait_all(copies):
    for copy in copies:
        copy.wait()


HBM = pl.BlockSpec(memory_space=pltpu.HBM)
SMEM = pl.BlockSpec(memory_space=pltpu.SMEM)
VMEM = pl.BlockSpec(memory_space=pltpu.VMEM)


def pack(view, chunk, count, place, carried, parts):
    per, _, half, lines = view.shape
    span = lines // 2
    width = span // count * 2
    depth = per * half
    quarter = half // 2
    steps = [(b, q * quarter) for q in range(2) for b in range(per)]

    def body(place_ref, v_ref, *refs):
        refs = list(refs)
        total = jnp.zeros((8, width), F32) if carried is None else refs.pop(0)[...]
        outs = [refs.pop(0) for _ in range(count if parts else 1)]
        sums, buf, packed, in_sem, out_sem = refs
        arrive = [
            pltpu.make_async_copy(
                v_ref.at[b, :, pl.ds(r, quarter), pl.ds(chunk * span, span)],
                buf.at[j],
                in_sem.at[j],
            )
            for j, (b, r) in enumerate(steps)
        ]
        for copy in arrive:
            copy.start()
        leave = []
        for j, (b, r) in enumerate(steps):
            arrive[j].wait()
            rows = pl.ds(j * quarter, quarter)
            for tile in range(count // 2):
                top = buf[j, 0, :, tile * width : (tile + 1) * width]
                low = buf[j, 1, :, tile * width : (tile + 1) * width]
                packed[2 * tile, rows, :] = merge(top, swap(low))
                packed[2 * tile + 1, rows, :] = merge(swap(top), low)
                square = top * top + low * low
                total += jnp.sum(square.reshape(quarter // 8, 8, width), axis=0)
            if not parts:
                leave.append(
                    pltpu.make_async_copy(packed.at[:, rows], outs[0].at[:, rows], out_sem.at[j])
                )
                leave[-1].start()
            elif b == per - 1:
                batch = far_copies(count, place_ref[0], packed, outs, out_sem, True, j // per)
                start_all(batch)
                leave += batch
        sums[...] = total
        wait_all(leave)

    if parts:
        outs = [jax.ShapeDtypeStruct((depth, width), F32)] * count
    else:
        outs = [jax.ShapeDtypeStruct((count, depth, width), F32)]
    result = pl.pallas_call(
        body,
        name="pack_pieces" if parts else "pack_stacked",
        in_specs=[SMEM, HBM] + [VMEM] * (carried is not None),
        out_specs=[HBM] * len(outs) + [VMEM],
        out_shape=outs + [jax.ShapeDtypeStruct((8, width), F32)],
        scratch_shapes=[
            pltpu.VMEM((len(steps), 2, quarter, span), F32),
            pltpu.VMEM((count, depth, width), F32),
            pltpu.SemaphoreType.DMA((len(steps),)),
            pltpu.SemaphoreType.DMA((max(2 * count, len(steps)),)),
        ],
        compiler_params=pltpu.CompilerParams(vmem_limit_bytes=58 << 20),
        cost_estimate=pl.CostEstimate(
            flops=depth * lines * 2, bytes_accessed=depth * lines * 8, transcendentals=0
        ),
    )(place, view, *([] if carried is None else [carried]))
    return (list(result[:count]) if parts else result[0]), result[-1]


def line_slopes(arrived, place, gram, tables, match, sums):
    gather = isinstance(arrived, list)
    below = 0 if sums is None else 8
    count = len(arrived) if gather else arrived.shape[0]
    depth, width = arrived[0].shape[-2:]
    slots, block = tables.shape[0], tables.shape[2] // 2
    half = block // 2
    quarter = half // 2
    per = depth // half
    out_blocks = per * count
    size = 2 * slots
    ext_rows = gram.shape[0]
    cuts = 4
    cut = slots // cuts

    def body(place_ref, g_ref, table_ref, *refs):
        refs = list(refs)
        sums_ref = refs.pop(0) if below else None
        ins = [refs.pop(0) for _ in range(count if gather else 1)]
        outs = [refs.pop(0) for _ in range(count)]
        t_ref, spec, extra, lines, result, table_sem, in_sem, out_sem, sum_sem = refs
        load = [
            pltpu.make_async_copy(
                table_ref.at[pl.ds(c * cut, cut)], t_ref.at[pl.ds(c * cut, cut)], table_sem.at[c]
            )
            for c in range(cuts)
        ]
        arrive = []
        for batch in range(2):
            rows = pl.ds(batch * per * quarter, per * quarter)
            if gather:
                arrive.append(far_copies(count, place_ref[0], lines, ins, in_sem, False, batch))
            else:
                arrive.append(
                    [
                        pltpu.make_async_copy(
                            ins[0].at[:, rows], lines.at[:, rows], in_sem.at[batch]
                        )
                    ]
                )
        start_all(arrive[1] + arrive[0] + load)

        def at_block(b, batch, at):
            row = (batch * per + b % per) * quarter
            return b // per, pl.ds(row + at, GROUP), slice(None)

        def forward(batch):
            def step(group, _):
                at = pl.multiple_of(group * GROUP, GROUP)
                here = pl.ds(batch * quarter + at, GROUP)
                seq = [lines[at_block(b, batch, at)] for b in range(out_blocks)]
                seq.append(extra[here, :])
                out = real_transform(seq + [None] * (size - out_blocks - 1))
                spec[0, here, :width] = out[0][0]
                spec[0, here, width:] = out[slots][0]
                for f in range(1, slots):
                    spec[f, here, :width] = out[f][0]
                    spec[f, here, width:] = out[f][1]
                return 0

            lax.fori_loop(0, quarter // GROUP, step, 0)

        extra[...] = jnp.zeros_like(extra)
        wait_all(arrive[1])
        early = ext_rows <= quarter
        if early:
            forward(1)
        wait_all(arrive[0])
        ext = jnp.zeros((ext_rows, width), F32)
        for j in range(match):
            ext += g_ref[:, j : j + 1] * lines[0, j : j + 1, :]
        for j in range(match):
            row = depth - match + j
            tail = swap(lines[count - 1, row : row + 1, :])
            ext += g_ref[:, match + j : match + j + 1] * tail
        extra[:ext_rows, :] = merge(ext, jnp.zeros_like(ext))

        forward(0)
        if not early:
            forward(1)
        wait_all(load)

        def product(f, blocks):
            high, mid, low = split_parts(jnp.concatenate(blocks, 0))
            one = jnp.dot(
                t_ref[f, : 2 * block, :],
                jnp.concatenate([high, mid], 1),
                preferred_element_type=F32,
            )
            two = jnp.dot(
                t_ref[f, block:, :],
                jnp.concatenate([low, high], 1),
                preferred_element_type=F32,
            )
            small = one[:block, width:] + (two[:block, :width] + two[block:, width:])
            got = one[block:, :width] + ((one[:block, :width] + one[block:, width:]) + small)
            top, bottom = got[:half], got[half:]
            spec[f, :, :width] = merge(top, swap(bottom))
            spec[f, :, width:] = merge(swap(top), bottom)

        re, im = spec[0, :, :width], spec[0, :, width:]
        none = jnp.zeros_like(re)
        product(
            0, [merge(re, none), merge(swap(re), none), merge(none, swap(im)), merge(none, im)]
        )

        def multiply(f, _):
            re, im = spec[f, :, :width], spec[f, :, width:]
            re_s, im_s = swap(re), swap(im)
            product(f, [merge(re, im_s), merge(re_s, im), merge(-im, re_s), merge(-im_s, re)])
            return 0

        lax.fori_loop(1, slots, multiply, 0, unroll=8)

        def backward(batch):
            def step(group, _):
                at = pl.multiple_of(group * GROUP, GROUP)
                here = pl.ds(batch * quarter + at, GROUP)
                values = [(spec[0, here, :width], None)]
                for f in range(1, slots):
                    values.append((spec[f, here, :width], spec[f, here, width:]))
                values.append((spec[0, here, width:], None))
                for b, value in enumerate(real_inverse(values, size, out_blocks)):
                    result[at_block(b, batch, at)] = value
                return 0

            lax.fori_loop(0, quarter // GROUP, step, 0)

        leave = []
        if below:
            for k in range(count):
                under = outs[k].at[pl.ds(depth, below)]
                leave.append(pltpu.make_async_copy(sums_ref, under, sum_sem.at[k]))
            start_all(leave)
        for batch in range(2):
            backward(batch)
            copies = far_copies(count, place_ref[0], result, outs, out_sem, True, batch)
            start_all(copies)
            leave += copies
        wait_all(leave)

    out_shape = [jax.ShapeDtypeStruct((depth + below, width), F32)] * count
    stacked = pltpu.VMEM((count, depth, width), F32)
    out = pl.pallas_call(
        body,
        name="line_slopes",
        in_specs=[SMEM, VMEM, HBM] + [VMEM] * (sums is not None) + [HBM] * (count if gather else 1),
        out_specs=[HBM] * len(out_shape),
        out_shape=out_shape,
        scratch_shapes=[
            pltpu.VMEM(tables.shape, BF),
            pltpu.VMEM((slots, half, 2 * width), F32),
            pltpu.VMEM((half, width), F32),
            stacked,
            stacked,
            pltpu.SemaphoreType.DMA((cuts,)),
            pltpu.SemaphoreType.DMA((2 * count,)),
            pltpu.SemaphoreType.DMA((2 * count,)),
            pltpu.SemaphoreType.DMA((count,)),
        ],
        compiler_params=pltpu.CompilerParams(vmem_limit_bytes=50 << 20),
        cost_estimate=pl.CostEstimate(
            flops=16 * size * block * block * width,
            bytes_accessed=8 * count * depth * width,
            transcendentals=0,
        ),
    )(place, gram, tables, *([sums] if below else []), *(arrived if gather else [arrived]))
    return list(out)


def advect(view, chunk, arrived, place, points, energy, earlier):
    adding = energy is None
    per, _, half, lines = view.shape
    span = lines // 2
    count = len(arrived)
    depth, width = per * half, arrived[0].shape[-1]
    quarter = half // 2
    steps = [(b, q * quarter) for q in range(2) for b in range(per)]
    kept = 0 if earlier is None else 2

    def body(place_ref, v_ref, *refs):
        refs = list(refs)[kept:]
        energy_in = None if adding else refs.pop(0)
        ins = [refs.pop(0) for _ in range(count)]
        s_ref, f_ref = refs.pop(0), refs.pop(0)
        energy_out = refs.pop(0) if adding else None
        v_buf, stacked, tiles, s_buf, f_buf, v_sem, in_sem, sum_sem, s_sem, f_sem = refs

        def part(ref, j):
            b, r = steps[j]
            return ref.at[b, :, pl.ds(r, quarter), pl.ds(chunk * span, span)]

        fields = [
            pltpu.make_async_copy(part(v_ref, j), v_buf.at[j], v_sem.at[j])
            for j in range(len(steps))
        ]
        pieces = [
            far_copies(count, place_ref[0], stacked, ins, in_sem, False, batch)
            for batch in range(2)
        ]
        below = []
        if adding:
            for k in range(count):
                under = ins[k].at[pl.ds(depth, 8)]
                below.append(pltpu.make_async_copy(under, tiles.at[k], sum_sem.at[k]))
        start_all(below + fields[:per] + pieces[0] + fields[per:] + pieces[1])
        wait_all(below)
        if adding:
            tile = tiles[0]
            for k in range(1, count):
                tile += tiles[k]
            energy_out[...] = tile
        else:
            tile = energy_in[...]
        lane_sum = jnp.sum(tile, axis=0, keepdims=True)
        mean_square = jnp.sum(lane_sum, axis=1, keepdims=True) / points
        rate = jnp.broadcast_to(courant / jnp.sqrt(mean_square + epsilon), (quarter, width))
        leave = []
        for j, (b, r) in enumerate(steps):
            if b == 0:
                wait_all(pieces[j // per])
            fields[j].wait()
            rows = pl.ds(j * quarter, quarter)
            for tile in range(count // 2):
                lanes = slice(tile * width, (tile + 1) * width)
                one = stacked[2 * tile, rows, :]
                two = stacked[2 * tile + 1, rows, :]
                for side, slope in enumerate((merge(one, swap(two)), merge(swap(one), two))):
                    field = v_buf[j, side, :, lanes]
                    s_buf[j, side, :, lanes] = slope
                    f_buf[j, side, :, lanes] = field - rate * field * slope
            leave.append(pltpu.make_async_copy(s_buf.at[j], part(s_ref, j), s_sem.at[j]))
            leave.append(pltpu.make_async_copy(f_buf.at[j], part(f_ref, j), f_sem.at[j]))
            start_all(leave[-2:])
        wait_all(leave)

    buffer = pltpu.VMEM((len(steps), 2, quarter, span), F32)
    step_sem = pltpu.SemaphoreType.DMA((len(steps),))
    piece_sem = pltpu.SemaphoreType.DMA((2 * count,))
    out = pl.pallas_call(
        body,
        name="advect",
        in_specs=[SMEM, HBM]
        + [HBM] * kept
        + [VMEM] * (not adding)
        + [HBM] * count,
        out_specs=[HBM, HBM] + [VMEM] * adding,
        out_shape=[jax.ShapeDtypeStruct(view.shape, F32)] * 2
        + [jax.ShapeDtypeStruct((8, width), F32)] * adding,
        scratch_shapes=[
            buffer,
            pltpu.VMEM((count, depth, width), F32),
            pltpu.VMEM((count, 8, width), F32),
            buffer,
            buffer,
            step_sem,
            piece_sem,
            piece_sem,
            step_sem,
            step_sem,
        ],
        input_output_aliases={2: 0, 3: 1} if kept else {},
        compiler_params=pltpu.CompilerParams(vmem_limit_bytes=12 << 20),
        cost_estimate=pl.CostEstimate(
            flops=depth * lines * 3, bytes_accessed=depth * lines * 16, transcendentals=0
        ),
    )(place, view, *(earlier or ()), *(() if adding else [energy]), *arrived)
    return out[:2], (out[2] if adding else energy)


def exchange(pieces, axis):
    if not isinstance(pieces, list):
        return lax.all_to_all(pieces, axis, split_axis=0, concat_axis=0, tiled=True)
    count = len(pieces)
    out = [pieces[0]]
    for k in range(1, count):
        moved = lax.ppermute(pieces[k], axis, [(i, (i + k) % count) for i in range(count)])
        out.append(moved)
    return out


def total_over(part, axis):
    size = lax.axis_size(axis)
    moving = part
    for _ in range(size - 1):
        moving = lax.ppermute(moving, axis, [(i, (i + 1) % size) for i in range(size)])
        part = part + moving
    return part


def per_device(velocity, left_gram, right_gram):
    row_count, line_total = velocity.shape
    cont, match = left_gram.shape
    gx_count = lax.axis_size("gx")
    ga_count = lax.axis_size("ga")
    place = lax.axis_index("gx").astype(jnp.int32).reshape(1)
    total = row_count * gx_count
    block = 2 * LANE
    while row_count % block or block > LANE:
        block //= 2
    half = block // 2
    assert cont <= half and match <= half and line_total % (gx_count * LANE) == 0
    out_blocks = total // block
    size = transform_size(2 * out_blocks)
    view = velocity.reshape(row_count // block, 2, half, line_total)

    points = row_count * line_total * gx_count * ga_count

    first, sums = pack(view, 0, gx_count, place, None, True)
    first = exchange(first, "gx")
    second, sums = pack(view, 1, gx_count, place, sums, False)
    sums = total_over(sums, "ga")
    spectrum = slope_spectrum(total + cont, block, out_blocks, size)
    tables = toeplitz_tables(jnp.asarray(spectrum), block)
    second, tables = lax.optimization_barrier((second, tables))
    second = exchange(second, "gx")
    gram = jnp.concatenate([left_gram, right_gram], axis=1)
    gram = jnp.pad(gram, ((0, -cont % 8), (0, 0)))
    first = line_slopes(first, place, gram, tables, match, sums)
    first = exchange(first, "gx")
    second = line_slopes(second, place, gram, tables, match, None)
    second = exchange(second, "gx")
    done, energy = advect(view, 0, first, place, points, None, None)
    done, _ = advect(view, 1, second, place, points, energy, done)
    return tuple(part.reshape(row_count, line_total) for part in done)


def solution(mesh):
    return jax.shard_map(
        per_device,
        mesh=mesh,
        in_specs=(P("gx", "ga"), P(), P()),
        out_specs=(P("gx", "ga"), P("gx", "ga")),
        check_vma=False,
    )
```

```python
import math

import jax
import jax.numpy as jnp
import numpy as np
from jax import lax
from jax.experimental import pallas as pl
from jax.experimental.pallas import tpu as pltpu
from jax.sharding import PartitionSpec as P

courant = 0.5
epsilon = 1e-06
LANE = 128
GROUP = 8
BF = jnp.bfloat16
F32 = jnp.float32


def add(a, b):
    return b if a is None else a if b is None else a + b


def sub(a, b):
    return a if b is None else -b if a is None else a - b


def scale(a, c):
    return None if a is None else a * np.float32(c)


def turn(value, angle):
    c, s = math.cos(angle), math.sin(angle)
    re, im = value
    return (sub(scale(re, c), scale(im, s)), add(scale(im, c), scale(re, s)))


def real_transform(seq):
    size = len(seq)
    if size == 1:
        return [(seq[0], None)]
    if size == 3:
        far = add(seq[1], seq[2])
        gap = sub(seq[1], seq[2])
        return [
            (add(seq[0], far), None),
            (sub(seq[0], scale(far, 0.5)), scale(gap, -math.sqrt(0.75))),
        ]
    even = real_transform(seq[0::2])
    odd = real_transform(seq[1::2])
    out = [None] * (size // 2 + 1)
    for f in range((size + 3) // 4):
        e = even[f]
        o = odd[f] if f == 0 else turn(odd[f], -2.0 * math.pi * f / size)
        out[f] = (add(e[0], o[0]), add(e[1], o[1]))
        out[size // 2 - f] = (sub(e[0], o[0]), sub(o[1], e[1]))
    if size % 4 == 0:
        f = size // 4
        out[f] = (even[f][0], scale(odd[f][0], -1.0))
    return out


def real_inverse(spec, size, count):
    if count <= 0:
        return []
    if size == 1:
        return [spec[0][0]]
    if size == 3:
        out = [add(spec[0][0], spec[1][0])]
        if count > 1:
            base = sub(spec[0][0], scale(spec[1][0], 0.5))
            side = scale(spec[1][1], math.sqrt(0.75))
            out.append(sub(base, side))
            out.append(add(base, side))
        return out[:count]
    half = size // 2
    even = [None] * (half // 2 + 1)
    odd = [None] * (half // 2 + 1)
    for f in range((size + 3) // 4):
        a, b = spec[f], spec[half - f]
        even[f] = (add(a[0], b[0]), sub(a[1], b[1]))
        diff = (sub(a[0], b[0]), add(a[1], b[1]))
        odd[f] = diff if f == 0 else turn(diff, 2.0 * math.pi * f / size)
    if size % 4 == 0:
        f = size // 4
        even[f] = (spec[f][0], None)
        odd[f] = (scale(spec[f][1], -1.0), None)
    first = real_inverse(even, half, (count + 1) // 2)
    second = real_inverse(odd, half, count // 2)
    out = [None] * count
    out[0::2] = first
    out[1::2] = second
    return out


def transform_size(least):
    size = 1
    while True:
        if size >= least:
            return size
        if size % 2 == 0 and size // 2 * 3 >= least:
            return size // 2 * 3
        size *= 2


def slope_spectrum(period, block, out_blocks, size):
    offsets = np.arange(size)
    offsets = np.where(offsets < out_blocks, offsets, offsets - size)
    step = np.arange(2 * block)
    index = block * offsets[:, None] + block - step[None, :]
    wrapped = (index + period // 2) % period - period // 2
    safe = np.where(wrapped == 0, 1, wrapped)
    sign = np.where(safe % 2 == 0, 1.0, -1.0)
    values = sign * (math.pi / period) / np.sin(math.pi * safe / period)
    values = np.where(wrapped == 0, 0.0, values)
    spectrum = np.fft.fft(values, axis=0)[: size // 2 + 1] / size
    table = np.empty((size, 2 * block))
    table[0] = spectrum[0].real
    table[1] = spectrum[size // 2].real
    table[2::2] = 2.0 * spectrum[1 : size // 2].real
    table[3::2] = 2.0 * spectrum[1 : size // 2].imag
    return table.astype(np.float32)


def split_parts(value):
    high = value.astype(BF)
    rest = value - high.astype(F32)
    mid = rest.astype(BF)
    return high, mid, (rest - mid.astype(F32)).astype(BF)


def left_lanes(shape):
    return lax.broadcasted_iota(jnp.int32, shape, len(shape) - 1) < shape[-1] // 2


def swap(value):
    return pltpu.roll(value, value.shape[-1] // 2, value.ndim - 1)


def merge(left, right):
    return jnp.where(left_lanes(left.shape), left, right)


def toeplitz_tables(spectrum, block):
    slots = spectrum.shape[0] // 2
    cuts = 4
    cut = slots // cuts

    def body(w_ref, o_ref, made, sem):
        def fill(f, _):
            for side in range(2):
                lane = w_ref[pl.ds(2 * f + side, 1), :]
                rows = jnp.broadcast_to(lane, (block, 2 * block))
                rows = pltpu.roll(rows, 0, 1, stride=1, stride_axis=0)[:, block:]
                high, mid, low = split_parts(rows)
                for p, part in enumerate((mid, high, low)):
                    made[f, p * block : (p + 1) * block, side * block : (side + 1) * block] = part
            return 0

        leave = []
        for c in range(cuts):
            lax.fori_loop(c * cut, (c + 1) * cut, fill, 0, unroll=4)
            part = pl.ds(c * cut, cut)
            leave.append(pltpu.make_async_copy(made.at[part], o_ref.at[part], sem.at[c]))
            leave[-1].start()
        for copy in leave:
            copy.wait()

    shape = (slots, 3 * block, 2 * block)
    return pl.pallas_call(
        body,
        name="toeplitz_tables",
        in_specs=[VMEM],
        out_specs=HBM,
        out_shape=jax.ShapeDtypeStruct(shape, BF),
        scratch_shapes=[pltpu.VMEM(shape, BF), pltpu.SemaphoreType.DMA((cuts,))],
        compiler_params=pltpu.CompilerParams(vmem_limit_bytes=58 << 20),
        cost_estimate=pl.CostEstimate(
            flops=slots * block * block * 32,
            bytes_accessed=slots * 3 * block * block * 4,
            transcendentals=0,
        ),
    )(spectrum)


def far_copies(count, place, stacked, pieces, sem, outward, batch):
    size = stacked.shape[1] // 2
    rows = pl.ds(batch * size, size)
    out = []
    for k in range(count):
        other = place + (k if outward else count - k)
        other = jnp.where(other >= count, other - count, other)
        mine = stacked.at[other, rows]
        piece = pieces[k].at[rows]
        pair = (mine, piece) if outward else (piece, mine)
        out.append(pltpu.make_async_copy(pair[0], pair[1], sem.at[batch * count + k]))
    return out


def start_all(copies):
    for copy in copies:
        copy.start()


def wait_all(copies):
    for copy in copies:
        copy.wait()


HBM = pl.BlockSpec(memory_space=pltpu.HBM)
SMEM = pl.BlockSpec(memory_space=pltpu.SMEM)
VMEM = pl.BlockSpec(memory_space=pltpu.VMEM)


def pack(view, chunk, count, place, carried, parts):
    per, _, half, lines = view.shape
    span = lines // 2
    width = span // count * 2
    depth = per * half
    quarter = half // 2
    steps = [(b, q * quarter) for q in range(2) for b in range(per)]

    def body(place_ref, v_ref, *refs):
        refs = list(refs)
        total = jnp.zeros((8, width), F32) if carried is None else refs.pop(0)[...]
        outs = [refs.pop(0) for _ in range(count if parts else 1)]
        sums, buf, packed, in_sem, out_sem = refs
        arrive = [
            pltpu.make_async_copy(
                v_ref.at[b, :, pl.ds(r, quarter), pl.ds(chunk * span, span)],
                buf.at[j],
                in_sem.at[j],
            )
            for j, (b, r) in enumerate(steps)
        ]
        for copy in arrive:
            copy.start()
        leave = []
        for j, (b, r) in enumerate(steps):
            arrive[j].wait()
            rows = pl.ds(j * quarter, quarter)
            for tile in range(count // 2):
                top = buf[j, 0, :, tile * width : (tile + 1) * width]
                low = buf[j, 1, :, tile * width : (tile + 1) * width]
                packed[2 * tile, rows, :] = merge(top, swap(low))
                packed[2 * tile + 1, rows, :] = merge(swap(top), low)
                square = top * top + low * low
                total += jnp.sum(square.reshape(quarter // 8, 8, width), axis=0)
            if not parts:
                leave.append(
                    pltpu.make_async_copy(packed.at[:, rows], outs[0].at[:, rows], out_sem.at[j])
                )
                leave[-1].start()
            elif b == per - 1:
                batch = far_copies(count, place_ref[0], packed, outs, out_sem, True, j // per)
                start_all(batch)
                leave += batch
        sums[...] = total
        wait_all(leave)

    if parts:
        outs = [jax.ShapeDtypeStruct((depth, width), F32)] * count
    else:
        outs = [jax.ShapeDtypeStruct((count, depth, width), F32)]
    result = pl.pallas_call(
        body,
        name="pack_pieces" if parts else "pack_stacked",
        in_specs=[SMEM, HBM] + [VMEM] * (carried is not None),
        out_specs=[HBM] * len(outs) + [VMEM],
        out_shape=outs + [jax.ShapeDtypeStruct((8, width), F32)],
        scratch_shapes=[
            pltpu.VMEM((len(steps), 2, quarter, span), F32),
            pltpu.VMEM((count, depth, width), F32),
            pltpu.SemaphoreType.DMA((len(steps),)),
            pltpu.SemaphoreType.DMA((max(2 * count, len(steps)),)),
        ],
        compiler_params=pltpu.CompilerParams(vmem_limit_bytes=58 << 20),
        cost_estimate=pl.CostEstimate(
            flops=depth * lines * 2, bytes_accessed=depth * lines * 8, transcendentals=0
        ),
    )(place, view, *([] if carried is None else [carried]))
    return (list(result[:count]) if parts else result[0]), result[-1]


def line_slopes(arrived, place, gram, tables, match, sums, spread):
    gather = isinstance(arrived, list)
    below = 0 if sums is None else 8
    count = len(arrived) if gather else arrived.shape[0]
    depth, width = arrived[0].shape[-2:]
    block = tables[0].shape[2] // 2
    slots = sum(table.shape[0] for table in tables)
    half = block // 2
    quarter = half // 2
    per = depth // half
    out_blocks = per * count
    size = 2 * slots
    ext_rows = gram.shape[0]
    held = len(tables)

    def body(place_ref, g_ref, *refs):
        refs = list(refs)
        table_refs = [refs.pop(0) for _ in range(held)]
        sums_ref = refs.pop(0) if below else None
        ins = [refs.pop(0) for _ in range(count if gather else 1)]
        outs = [refs.pop(0) for _ in range(count if spread else 1)]
        t_ref, spec, extra, lines, result, table_sem, in_sem, out_sem, sum_sem = refs
        load = []
        for c, table_ref in enumerate(table_refs):
            first = sum(table.shape[0] for table in tables[:c])
            into = t_ref.at[pl.ds(first, tables[c].shape[0])]
            load.append(pltpu.make_async_copy(table_ref, into, table_sem.at[c]))
        arrive = []
        for batch in range(2):
            rows = pl.ds(batch * per * quarter, per * quarter)
            if gather:
                arrive.append(far_copies(count, place_ref[0], lines, ins, in_sem, False, batch))
            else:
                arrive.append(
                    [
                        pltpu.make_async_copy(
                            ins[0].at[:, rows], lines.at[:, rows], in_sem.at[batch]
                        )
                    ]
                )
        start_all(arrive[1] + arrive[0] + load)

        def at_block(b, batch, at):
            row = (batch * per + b % per) * quarter
            return b // per, pl.ds(row + at, GROUP), slice(None)

        def forward(batch):
            def step(group, _):
                at = pl.multiple_of(group * GROUP, GROUP)
                here = pl.ds(batch * quarter + at, GROUP)
                seq = [lines[at_block(b, batch, at)] for b in range(out_blocks)]
                seq.append(extra[here, :])
                out = real_transform(seq + [None] * (size - out_blocks - 1))
                spec[0, here, :width] = out[0][0]
                spec[0, here, width:] = out[slots][0]
                for f in range(1, slots):
                    spec[f, here, :width] = out[f][0]
                    spec[f, here, width:] = out[f][1]
                return 0

            lax.fori_loop(0, quarter // GROUP, step, 0)

        extra[...] = jnp.zeros_like(extra)
        wait_all(arrive[1])
        early = ext_rows <= quarter
        if early:
            forward(1)
        wait_all(arrive[0])
        ext = jnp.zeros((ext_rows, width), F32)
        for j in range(match):
            ext += g_ref[:, j : j + 1] * lines[0, j : j + 1, :]
        for j in range(match):
            row = depth - match + j
            tail = swap(lines[count - 1, row : row + 1, :])
            ext += g_ref[:, match + j : match + j + 1] * tail
        extra[:ext_rows, :] = merge(ext, jnp.zeros_like(ext))

        forward(0)
        if not early:
            forward(1)
        wait_all(load)

        def product(f, blocks):
            high, mid, low = split_parts(jnp.concatenate(blocks, 0))
            one = jnp.dot(
                t_ref[f, : 2 * block, :],
                jnp.concatenate([high, mid], 1),
                preferred_element_type=F32,
            )
            two = jnp.dot(
                t_ref[f, block:, :],
                jnp.concatenate([low, high], 1),
                preferred_element_type=F32,
            )
            small = one[:block, width:] + (two[:block, :width] + two[block:, width:])
            got = one[block:, :width] + ((one[:block, :width] + one[block:, width:]) + small)
            top, bottom = got[:half], got[half:]
            spec[f, :, :width] = merge(top, swap(bottom))
            spec[f, :, width:] = merge(swap(top), bottom)

        re, im = spec[0, :, :width], spec[0, :, width:]
        none = jnp.zeros_like(re)
        product(
            0, [merge(re, none), merge(swap(re), none), merge(none, swap(im)), merge(none, im)]
        )

        def multiply(f, _):
            re, im = spec[f, :, :width], spec[f, :, width:]
            re_s, im_s = swap(re), swap(im)
            product(f, [merge(re, im_s), merge(re_s, im), merge(-im, re_s), merge(-im_s, re)])
            return 0

        lax.fori_loop(1, slots, multiply, 0, unroll=8)

        def backward(batch):
            def step(group, _):
                at = pl.multiple_of(group * GROUP, GROUP)
                here = pl.ds(batch * quarter + at, GROUP)
                values = [(spec[0, here, :width], None)]
                for f in range(1, slots):
                    values.append((spec[f, here, :width], spec[f, here, width:]))
                values.append((spec[0, here, width:], None))
                for b, value in enumerate(real_inverse(values, size, out_blocks)):
                    result[at_block(b, batch, at)] = value
                return 0

            lax.fori_loop(0, quarter // GROUP, step, 0)

        leave = []
        if below:
            for k in range(count):
                under = outs[k].at[pl.ds(depth, below)]
                leave.append(pltpu.make_async_copy(sums_ref, under, sum_sem.at[k]))
            start_all(leave)
        for batch in range(2):
            backward(batch)
            if spread:
                copies = far_copies(count, place_ref[0], result, outs, out_sem, True, batch)
            else:
                rows = pl.ds(batch * per * quarter, per * quarter)
                source, target = result.at[:, rows], outs[0].at[:, rows]
                copies = [pltpu.make_async_copy(source, target, out_sem.at[batch])]
            start_all(copies)
            leave += copies
        wait_all(leave)

    if spread:
        out_shape = [jax.ShapeDtypeStruct((depth + below, width), F32)] * count
    else:
        out_shape = [jax.ShapeDtypeStruct((count, depth, width), F32)]
    stacked = pltpu.VMEM((count, depth, width), F32)
    out = pl.pallas_call(
        body,
        name="line_slopes",
        in_specs=[SMEM, VMEM] + [HBM] * held + [VMEM] * (sums is not None) + [HBM] * (count if gather else 1),
        out_specs=[HBM] * len(out_shape),
        out_shape=out_shape,
        scratch_shapes=[
            pltpu.VMEM((slots, *tables[0].shape[1:]), BF),
            pltpu.VMEM((slots, half, 2 * width), F32),
            pltpu.VMEM((half, width), F32),
            stacked,
            stacked,
            pltpu.SemaphoreType.DMA((held,)),
            pltpu.SemaphoreType.DMA((2 * count,)),
            pltpu.SemaphoreType.DMA((2 * count,)),
            pltpu.SemaphoreType.DMA((count,)),
        ],
        compiler_params=pltpu.CompilerParams(vmem_limit_bytes=50 << 20),
        cost_estimate=pl.CostEstimate(
            flops=16 * size * block * block * width,
            bytes_accessed=8 * count * depth * width,
            transcendentals=0,
        ),
    )(place, gram, *tables, *([sums] if below else []), *(arrived if gather else [arrived]))
    return list(out) if spread else out[0]


def advect(view, chunk, arrived, place, points, energy, earlier):
    adding = energy is None
    gather = isinstance(arrived, list)
    per, _, half, lines = view.shape
    span = lines // 2
    count = len(arrived)
    depth, width = per * half, arrived[0].shape[-1]
    quarter = half // 2
    steps = [(b, q * quarter) for q in range(2) for b in range(per)]
    kept = 0 if earlier is None else 2

    def body(place_ref, v_ref, *refs):
        refs = list(refs)[kept:]
        energy_in = None if adding else refs.pop(0)
        ins = [refs.pop(0) for _ in range(count if gather else 1)]
        s_ref, f_ref = refs.pop(0), refs.pop(0)
        energy_out = refs.pop(0) if adding else None
        v_buf, stacked, tiles, s_buf, f_buf, v_sem, in_sem, sum_sem, s_sem, f_sem = refs

        def part(ref, j):
            b, r = steps[j]
            return ref.at[b, :, pl.ds(r, quarter), pl.ds(chunk * span, span)]

        fields = [
            pltpu.make_async_copy(part(v_ref, j), v_buf.at[j], v_sem.at[j])
            for j in range(len(steps))
        ]
        pieces = []
        for batch in range(2):
            if gather:
                pieces.append(
                    far_copies(count, place_ref[0], stacked, ins, in_sem, False, batch)
                )
            else:
                rows = pl.ds(batch * per * quarter, per * quarter)
                source, target = ins[0].at[:, rows], stacked.at[:, rows]
                pieces.append([pltpu.make_async_copy(source, target, in_sem.at[batch])])
        below = []
        if adding:
            for k in range(count):
                under = ins[k].at[pl.ds(depth, 8)]
                below.append(pltpu.make_async_copy(under, tiles.at[k], sum_sem.at[k]))
        start_all(below + pieces[0] + fields[:per] + pieces[1] + fields[per:])
        wait_all(below)
        if adding:
            tile = tiles[0]
            for k in range(1, count):
                tile += tiles[k]
            energy_out[...] = tile
        else:
            tile = energy_in[...]
        lane_sum = jnp.sum(tile, axis=0, keepdims=True)
        mean_square = jnp.sum(lane_sum, axis=1, keepdims=True) / points
        rate = jnp.broadcast_to(courant / jnp.sqrt(mean_square + epsilon), (quarter, width))
        leave = []
        for j, (b, r) in enumerate(steps):
            if b == 0:
                wait_all(pieces[j // per])
            fields[j].wait()
            rows = pl.ds(j * quarter, quarter)
            for tile in range(count // 2):
                lanes = slice(tile * width, (tile + 1) * width)
                one = stacked[2 * tile, rows, :]
                two = stacked[2 * tile + 1, rows, :]
                for side, slope in enumerate((merge(one, swap(two)), merge(swap(one), two))):
                    field = v_buf[j, side, :, lanes]
                    s_buf[j, side, :, lanes] = slope
                    f_buf[j, side, :, lanes] = field - rate * field * slope
            leave.append(pltpu.make_async_copy(s_buf.at[j], part(s_ref, j), s_sem.at[j]))
            leave.append(pltpu.make_async_copy(f_buf.at[j], part(f_ref, j), f_sem.at[j]))
            start_all(leave[-2:])
        wait_all(leave)

    buffer = pltpu.VMEM((len(steps), 2, quarter, span), F32)
    step_sem = pltpu.SemaphoreType.DMA((len(steps),))
    piece_sem = pltpu.SemaphoreType.DMA((2 * count,))
    out = pl.pallas_call(
        body,
        name="advect",
        in_specs=[SMEM, HBM]
        + [HBM] * kept
        + [VMEM] * (not adding)
        + [HBM] * (count if gather else 1),
        out_specs=[HBM, HBM] + [VMEM] * adding,
        out_shape=[jax.ShapeDtypeStruct(view.shape, F32)] * 2
        + [jax.ShapeDtypeStruct((8, width), F32)] * adding,
        scratch_shapes=[
            buffer,
            pltpu.VMEM((count, depth, width), F32),
            pltpu.VMEM((count, 8, width), F32),
            buffer,
            buffer,
            step_sem,
            piece_sem,
            piece_sem,
            step_sem,
            step_sem,
        ],
        input_output_aliases={2: 0, 3: 1} if kept else {},
        compiler_params=pltpu.CompilerParams(vmem_limit_bytes=12 << 20),
        cost_estimate=pl.CostEstimate(
            flops=depth * lines * 3, bytes_accessed=depth * lines * 16, transcendentals=0
        ),
    )(place, view, *(earlier or ()), *(() if adding else [energy]), *(arrived if gather else [arrived]))
    return out[:2], (out[2] if adding else energy)


def exchange(pieces, axis):
    if not isinstance(pieces, list):
        return lax.all_to_all(pieces, axis, split_axis=0, concat_axis=0, tiled=True)
    count = len(pieces)
    out = [pieces[0]]
    for k in range(1, count):
        moved = lax.ppermute(pieces[k], axis, [(i, (i + k) % count) for i in range(count)])
        out.append(moved)
    return out


def total_over(part, axis):
    size = lax.axis_size(axis)
    moving = part
    for _ in range(size - 1):
        moving = lax.ppermute(moving, axis, [(i, (i + 1) % size) for i in range(size)])
        part = part + moving
    return part


def per_device(velocity, left_gram, right_gram):
    row_count, line_total = velocity.shape
    cont, match = left_gram.shape
    gx_count = lax.axis_size("gx")
    ga_count = lax.axis_size("ga")
    place = lax.axis_index("gx").astype(jnp.int32).reshape(1)
    total = row_count * gx_count
    block = 2 * LANE
    while row_count % block or block > LANE:
        block //= 2
    half = block // 2
    assert cont <= half and match <= half and line_total % (gx_count * LANE) == 0
    out_blocks = total // block
    size = transform_size(2 * out_blocks)
    view = velocity.reshape(row_count // block, 2, half, line_total)

    points = row_count * line_total * gx_count * ga_count

    spectrum = slope_spectrum(total + cont, block, out_blocks, size)
    cut = size // 4 * 2
    spectra = [jnp.asarray(part) for part in (spectrum[:cut], spectrum[cut:])]

    first, sums = pack(view, 0, gx_count, place, None, True)
    first = exchange(first, "gx")
    second, sums = pack(view, 1, gx_count, place, sums, False)
    tables = [toeplitz_tables(spectra[0], block)]
    second, tables[0] = lax.optimization_barrier((second, tables[0]))
    second = exchange(second, "gx")
    sums = total_over(sums, "ga")
    tables.append(toeplitz_tables(spectra[1], block))
    gram = jnp.concatenate([left_gram, right_gram], axis=1)
    gram = jnp.pad(gram, ((0, -cont % 8), (0, 0)))
    first = line_slopes(first, place, gram, tables, match, sums, True)
    first = exchange(first, "gx")
    second = line_slopes(second, place, gram, tables, match, None, True)
    second = exchange(second, "gx")
    done, energy = advect(view, 0, first, place, points, None, None)
    done, _ = advect(view, 1, second, place, points, energy, done)
    return tuple(part.reshape(row_count, line_total) for part in done)


def solution(mesh):
    return jax.shard_map(
        per_device,
        mesh=mesh,
        in_specs=(P("gx", "ga"), P(), P()),
        out_specs=(P("gx", "ga"), P("gx", "ga")),
        check_vma=False,
    )
```
